256 devices in a mesh: space: 8 (over x, core), mem: 32 (over z, y).
Axes of the slice: x: 4, y: 4, z: 8, core: 2. Of those that a mesh axis runs over, the one named last changes fastest.
Arguments:
- prior_ensemble: float32 [512, 65536], P('mem', 'space'), may hold values from -5 to 5
- terminal_particles: float32 [512, 65536], P(None, ('space', 'mem')), may hold values from -5 to 5
- reverse_perturbation: float32 [3, 512, 65536], P(None, None, ('space', 'mem')), may hold values from -6 to 6
- measured_angles: float32 [65536], P(('space', 'mem')), may hold values from -1.3 to 1.3
Outputs:
- analysis: float32 [512, 65536], P(None, ('space', 'mem'))
The draws below stay inside these ranges and needn't reach their ends.
All inputs are finite; a program needn't handle non-finite values.
Results may differ from the reference program's by a relative error of at most 0.0003.
Values sent between devices are 32-bit elements; how exact they have to be, the bound alone decides.
No kernel may reach another device: no remote copies, remote signals or barrier semaphores. Data moves between devices by JAX's collectives and lax.ppermute only.
A program may use at most 64 MiB of HBM per device.

```python
import math
import jax
import jax.numpy as jnp
from jax import lax

M = 512
S = 512
ITERS = 3
V = 65536


def member_field(key):
    base = jax.random.fold_in(key, 7)
    first = jax.random.fold_in(base, 0)
    return jnp.clip(jax.random.normal(first, (M, V), jnp.float32), -5.0, 5.0)


def draw_prior_ensemble(key, part):
    return member_field(key).astype(jnp.float32)


def draw_terminal_particles(key, part):
    base = jax.random.fold_in(key, 11)
    return jnp.clip(jax.random.normal(base, (S, V), jnp.float32), -5.0, 5.0)


def block_levels(rng, extent, pieces, low, largest):
    def one(position, shards_of):
        steps = jax.random.uniform(jax.random.fold_in(jax.random.fold_in(rng, 6), position), (shards_of,), jnp.float32, low / len(pieces), largest / len(pieces))
        return jnp.repeat(jnp.exp(steps), extent[position] // shards_of).reshape((-1,) + (1,) * (len(extent) - position - 1))

    factor_of = one(*pieces[0])
    for cut in pieces[1:]:
        factor_of = factor_of * one(*cut)
    return factor_of


def noise(key, shape, scale, reach, pieces=(), kind=jnp.bfloat16):
    array = scale * jax.random.normal(key, shape, jnp.float32)
    if pieces:
        array = array * block_levels(key, shape, pieces, -0.22, 0.18)
    return jnp.clip(array, -reach, reach).astype(kind)


def setup_inputs(seed: int = 0) -> dict:
    key_list = jax.random.split(jax.random.key(seed), 5)
    prior_ensemble = draw_prior_ensemble(jax.random.fold_in(key_list[4], 71), 0)
    terminal_particles = draw_terminal_particles(jax.random.fold_in(key_list[4], 71), 0)
    reverse_perturbation = noise(key_list[2], (ITERS, S, V), 1.0, 6.0, ((2, 256),), jnp.float32)
    measured_angles = jnp.clip(jax.random.uniform(key_list[3], (V,), jnp.float32, -1.3, 1.3) * block_levels(key_list[3], (V,), ((0, 256),), -0.4, 0.0), -1.3, 1.3)
    return {"prior_ensemble": prior_ensemble, "terminal_particles": terminal_particles, "reverse_perturbation": reverse_perturbation, "measured_angles": measured_angles}


def reference(prior_ensemble, terminal_particles, reverse_perturbation, measured_angles):
    peak_log_likelihood = lax.Precision.HIGHEST
    particle_lengths = lax.optimization_barrier(jnp.sum(prior_ensemble * prior_ensemble, axis=1))
    temper = math.sqrt(V)
    gaussian_variates = terminal_particles
    for step in range(ITERS):
        t = 1.0 - step / ITERS
        dt = 1.0 / ITERS
        alpha = 1.0 - 0.5 * t
        sigma2 = t
        drift = -0.5 / alpha
        g2 = 1.0 + t / alpha
        damp = 1.0 - t
        inner_pairing_matrix = jnp.dot(gaussian_variates, prior_ensemble.T, precision=peak_log_likelihood, preferred_element_type=jnp.float32)
        logits = (2.0 * alpha * inner_pairing_matrix - alpha * alpha * particle_lengths[None, :]) / (2.0 * sigma2 * temper)
        annealed_importance = jax.nn.softmax(logits, axis=1)
        mixed_correction = jnp.dot(annealed_importance, prior_ensemble, precision=peak_log_likelihood, preferred_element_type=jnp.float32)
        score = -(gaussian_variates - alpha * mixed_correction) / sigma2 + damp * 4.0 * (measured_angles[None, :] - jnp.arctan(gaussian_variates)) / (1.0 + gaussian_variates * gaussian_variates)
        gaussian_variates = gaussian_variates + dt * (-drift * gaussian_variates + g2 * score) + math.sqrt(dt * g2) * reverse_perturbation[step]
    return gaussian_variates
```

```python
import math

import jax
import jax.numpy as jnp
from jax import lax
from jax.sharding import PartitionSpec as P

ITERS = 3
STREAMS = 1
AXES = ("space", "mem")


def half(array, which, axis):
    size = array.shape[axis] // 2
    return lax.dynamic_slice_in_dim(array, which * size, size, axis)


def per_device(prior_ensemble, terminal_particles, reverse_perturbation, measured_angles):
    space, mem = lax.axis_size("space"), lax.axis_size("mem")
    core = lax.rem(lax.axis_index("space"), 2)
    swap = [(i, i ^ 1) for i in range(space)]
    groups = [
        [s * mem + m for s in range(c, space, 2) for m in range(mem)] for c in range(2)
    ]
    peers = len(groups[0])
    precision = lax.Precision.HIGHEST

    def pair_up(array, axis):
        other = lax.ppermute(half(array, 1 - core, axis), "space", swap)
        return jnp.concatenate([half(array, core, axis), other], axis=-1)

    exchange = lambda a: lax.all_to_all(
        a, AXES, split_axis=0, concat_axis=0, tiled=True, axis_index_groups=groups
    )

    mine = lax.all_to_all(prior_ensemble, "mem", split_axis=1, concat_axis=0, tiled=True)
    members = jnp.concatenate([mine, lax.ppermute(mine, "space", swap)], axis=1)
    particles = pair_up(terminal_particles, 0)
    perturbation = pair_up(reverse_perturbation, 1)
    angles = jnp.concatenate(
        [measured_angles, lax.ppermute(measured_angles, "space", swap)]
    )
    temper = math.sqrt(measured_angles.shape[0] * space * mem)
    lengths = jnp.sum(members * members, axis=1)

    count = particles.shape[0] // STREAMS
    states = [particles[i * count : (i + 1) * count] for i in range(STREAMS)]
    for step in range(ITERS):
        t = 1.0 - step / ITERS
        dt = 1.0 / ITERS
        alpha = 1.0 - 0.5 * t
        drift = -0.5 / alpha
        g2 = 1.0 + t / alpha
        damp = 1.0 - t
        for i in range(STREAMS):
            z = states[i]
            gram = jnp.einsum(
                "sv,mv->sm",
                z,
                members,
                precision=precision,
                preferred_element_type=jnp.float32,
            )
            partial = (2.0 * alpha * gram - alpha * alpha * lengths[None, :]) / (
                2.0 * t * temper
            )
            received = exchange(partial)
            logits = jnp.sum(received.reshape(peers, count // peers, -1), axis=0)
            weights = jax.nn.softmax(logits, axis=1)
            weights = exchange(
                jnp.broadcast_to(weights[None], (peers,) + weights.shape).reshape(
                    count, -1
                )
            )
            noise = perturbation[step, i * count : (i + 1) * count]
            pull = damp * 4.0 * (angles[None, :] - jnp.arctan(z)) / (1.0 + z * z)
            rest = (
                z
                + dt * (-drift * z + g2 * (pull - z / t))
                + math.sqrt(dt * g2) * noise
            )
            blend = jnp.dot(
                weights,
                members,
                precision=precision,
                preferred_element_type=jnp.float32,
            )
            states[i] = rest + (dt * g2 * alpha / t) * blend
    z = jnp.concatenate(states, axis=0)
    width = measured_angles.shape[0]
    back = lax.ppermute(z[:, width:], "space", swap)
    kept = z[:, :width]
    first = core == 0
    return jnp.concatenate(
        [jnp.where(first, kept, back), jnp.where(first, back, kept)], axis=0
    )


def solution(mesh):
    in_specs = (
        P("mem", "space"),
        P(None, ("space", "mem")),
        P(None, None, ("space", "mem")),
        P(("space", "mem")),
    )
    out_specs = P(None, ("space", "mem"))
    return jax.shard_map(
        per_device, mesh=mesh, in_specs=in_specs, out_specs=out_specs, check_vma=False
    )
```

```python
import math

import jax
import jax.numpy as jnp
from jax import lax
from jax.sharding import PartitionSpec as P

ITERS = 3
AXES = ("space", "mem")


def half(array, which, axis):
    size = array.shape[axis] // 2
    return lax.dynamic_slice_in_dim(array, which * size, size, axis)


def per_device(prior_ensemble, terminal_particles, reverse_perturbation, measured_angles):
    space, mem = lax.axis_size("space"), lax.axis_size("mem")
    core = lax.rem(lax.axis_index("space"), 2)
    swap = [(i, i ^ 1) for i in range(space)]
    depth = 8
    width = mem // depth
    planes = [
        [s * mem + z * width + y for s in range(c, space, 2) for y in range(width)]
        for c in range(2)
        for z in range(depth)
    ]
    columns = [[z * width + y for z in range(depth)] for y in range(width)]
    peers = len(planes[0])
    precision = lax.Precision.HIGHEST

    def pair_up(array, axis):
        other = lax.ppermute(half(array, 1 - core, axis), "space", swap)
        return jnp.concatenate([half(array, core, axis), other], axis=-1)

    def in_plane(blocks):
        return lax.all_to_all(
            blocks, AXES, split_axis=0, concat_axis=0, axis_index_groups=planes
        )

    def in_column(blocks):
        return lax.all_to_all(
            blocks, "mem", split_axis=0, concat_axis=0, axis_index_groups=columns
        )

    own = lax.all_to_all(prior_ensemble, "mem", split_axis=1, concat_axis=0, tiled=True)
    members = jnp.concatenate([own, lax.ppermute(own, "space", swap)], axis=1)
    particles = pair_up(terminal_particles, 0)
    perturbation = pair_up(reverse_perturbation, 1)
    angles = jnp.concatenate(
        [measured_angles, lax.ppermute(measured_angles, "space", swap)]
    )
    temper = math.sqrt(measured_angles.shape[0] * space * mem)
    lengths = jnp.sum(members * members, axis=1)

    z = particles
    count, total = z.shape[0], members.shape[0]
    rows = count // peers
    for step in range(ITERS):
        t = 1.0 - step / ITERS
        dt = 1.0 / ITERS
        alpha = 1.0 - 0.5 * t
        drift = -0.5 / alpha
        g2 = 1.0 + t / alpha
        damp = 1.0 - t
        gram = jnp.einsum(
            "sv,mv->sm",
            z,
            members,
            precision=precision,
            preferred_element_type=jnp.float32,
        )
        partial = (2.0 * alpha * gram - alpha * alpha * lengths[None, :]) / (
            2.0 * t * temper
        )
        plane_sum = jnp.sum(in_plane(partial.reshape(peers, rows, total)), axis=0)
        spread = jnp.broadcast_to(plane_sum[None], (depth, rows, total))
        logits = jnp.sum(in_column(spread), axis=0)
        weights = jax.nn.softmax(logits, axis=1)
        weights = in_plane(jnp.broadcast_to(weights[None], (peers, rows, total)))
        pull = damp * 4.0 * (angles[None, :] - jnp.arctan(z)) / (1.0 + z * z)
        rest = (
            z
            + dt * (-drift * z + g2 * (pull - z / t))
            + math.sqrt(dt * g2) * perturbation[step]
        )
        blend = jnp.dot(
            weights.reshape(count, total),
            members,
            precision=precision,
            preferred_element_type=jnp.float32,
        )
        z = rest + (dt * g2 * alpha / t) * blend
    mine = measured_angles.shape[0]
    back = lax.ppermute(z[:, mine:], "space", swap)
    kept = z[:, :mine]
    first = core == 0
    return jnp.concatenate(
        [jnp.where(first, kept, back), jnp.where(first, back, kept)], axis=0
    )


def solution(mesh):
    in_specs = (
        P("mem", "space"),
        P(None, ("space", "mem")),
        P(None, None, ("space", "mem")),
        P(("space", "mem")),
    )
    out_specs = P(None, ("space", "mem"))
    return jax.shard_map(
        per_device, mesh=mesh, in_specs=in_specs, out_specs=out_specs, check_vma=False
    )
```

```python
import math

import jax
import jax.numpy as jnp
from jax import lax
from jax.sharding import PartitionSpec as P

ITERS = 3
DEPTH = 8
AXES = ("space", "mem")


def constants(step):
    t = 1.0 - step / ITERS
    dt = 1.0 / ITERS
    alpha = 1.0 - 0.5 * t
    drift = -0.5 / alpha
    g2 = 1.0 + t / alpha
    damp = 1.0 - t
    keep = 1.0 - dt * drift - dt * g2 / t
    gain = dt * g2 * alpha / t
    pull = dt * g2 * damp * 4.0
    noise = math.sqrt(dt * g2)
    return alpha, t, keep, gain, pull, noise


def product(a, b, contract):
    return lax.dot_general(
        a,
        b,
        (contract, ((), ())),
        precision=lax.Precision.HIGHEST,
        preferred_element_type=jnp.float32,
    )


def half(array, which, axis):
    size = array.shape[axis] // 2
    return lax.dynamic_slice_in_dim(array, which * size, size, axis)


def per_device(prior_ensemble, terminal_particles, reverse_perturbation, measured_angles):
    space, mem = lax.axis_size("space"), lax.axis_size("mem")
    core = lax.rem(lax.axis_index("space"), 2)
    swap = [(i, i ^ 1) for i in range(space)]
    width = mem // DEPTH
    planes = [
        [s * mem + z * width + y for s in range(c, space, 2) for y in range(width)]
        for c in range(2)
        for z in range(DEPTH)
    ]
    columns = [[z * width + y for z in range(DEPTH)] for y in range(width)]
    peers = len(planes[0])

    def other_core(array):
        return lax.ppermute(array, "space", swap)

    def pair_up(array):
        return jnp.concatenate(
            [half(array, core, 0), other_core(half(array, 1 - core, 0))], axis=1
        )

    def in_plane(blocks):
        return lax.all_to_all(
            blocks, AXES, split_axis=0, concat_axis=0, axis_index_groups=planes
        )

    def column_sum(block):
        spread = jnp.broadcast_to(block[None], (DEPTH,) + block.shape)
        return jnp.sum(
            lax.all_to_all(
                spread, "mem", split_axis=0, concat_axis=0, axis_index_groups=columns
            ),
            axis=0,
        )

    def to_all(block):
        return jnp.broadcast_to(block[None], (peers,) + block.shape)

    temper = math.sqrt(measured_angles.shape[0] * space * mem)
    a0, t0, keep0, gain0, pull0, noise0 = constants(0)
    a1, t1, keep1, gain1, pull1, noise1 = constants(1)
    a2, t2, keep2, gain2, pull2, noise2 = constants(2)

    z0 = pair_up(terminal_particles)
    e0, e1, e2 = (pair_up(reverse_perturbation[step]) for step in range(ITERS))
    angles = jnp.concatenate([measured_angles, other_core(measured_angles)])[None, :]

    def misfit(z):
        return (angles - jnp.arctan(z)) / (1.0 + z * z)

    u0 = keep0 * z0 + pull0 * misfit(z0) + noise0 * e0

    own = lax.all_to_all(prior_ensemble, "mem", split_axis=1, concat_axis=0, tiled=True)
    members = jnp.concatenate([own, other_core(own)], axis=1)
    count, total = z0.shape[0], members.shape[0]
    rows = count // peers

    def by_row_owner(array):
        return array.reshape(peers, rows, array.shape[-1])

    lengths = jnp.sum(members * members, axis=1)[None, None, :]
    stack = jnp.concatenate(
        [by_row_owner(z0), by_row_owner(u0), by_row_owner(half(members, core, 0))],
        axis=1,
    )
    partial = product(
        stack.reshape(3 * count, -1), members, ((1,), (1,))
    ).reshape(peers, 3, rows, total)
    partial = jnp.stack(
        [
            2.0 * a0 * partial[:, 0] - a0 * a0 * lengths,
            2.0 * a1 * partial[:, 1] - a1 * a1 * lengths,
            partial[:, 2],
        ],
        axis=1,
    )
    sums = column_sum(jnp.sum(in_plane(partial), axis=0))
    raw0, raw1, pairs = sums[0], sums[1], sums[2]
    w0 = jax.nn.softmax(raw0 / (2.0 * t0 * temper), axis=1)
    got = in_plane(to_all(jnp.stack([w0, pairs])))
    weights0 = got[:, 0].reshape(count, total)
    near = got[:, 1].reshape(count, total)
    far = other_core(near)

    z1 = u0 + gain0 * product(weights0, members, ((1,), (0,)))
    v1 = pull1 * misfit(z1) + noise1 * e1
    v1_members = product(v1, members, ((1,), (1,)))

    def times_pairs(w):
        return product(half(w, core, 1), near, ((1,), (0,))) + product(
            half(w, 1 - core, 1), far, ((1,), (0,))
        )

    w0_pairs = times_pairs(w0)
    raw1 = raw1 + (2.0 * a1 * gain0) * w0_pairs
    w1 = jax.nn.softmax(raw1 / (2.0 * t1 * temper), axis=1)

    partial = by_row_owner(
        2.0 * a2 * v1_members + (a2 * keep1 * a1 - a2 * a2) * lengths[0]
    )
    got = in_plane(jnp.stack([partial, to_all(w1)], axis=1))
    weights1 = got[:, 1].reshape(count, total)
    raw2 = column_sum(jnp.sum(got[:, 0], axis=0))
    raw2 = raw2 + (a2 * keep1 / a1) * raw1 + (2.0 * a2 * gain1) * times_pairs(w1)
    w2 = jax.nn.softmax(raw2 / (2.0 * t2 * temper), axis=1)
    weights2 = in_plane(to_all(w2)).reshape(count, total)

    z2 = keep1 * z1 + v1 + gain1 * product(weights1, members, ((1,), (0,)))
    u2 = keep2 * z2 + pull2 * misfit(z2) + noise2 * e2
    u2 = lax.optimization_barrier(u2)
    z3 = u2 + gain2 * product(weights2, members, ((1,), (0,)))

    mine = measured_angles.shape[0]
    kept, back = z3[:, :mine], other_core(z3[:, mine:])
    first = core == 0
    return jnp.concatenate(
        [jnp.where(first, kept, back), jnp.where(first, back, kept)], axis=0
    )


def solution(mesh):
    in_specs = (
        P("mem", "space"),
        P(None, ("space", "mem")),
        P(None, None, ("space", "mem")),
        P(("space", "mem")),
    )
    out_specs = P(None, ("space", "mem"))
    return jax.shard_map(
        per_device, mesh=mesh, in_specs=in_specs, out_specs=out_specs, check_vma=False
    )
```

```python
import math

import jax
import jax.numpy as jnp
from jax import lax
from jax.sharding import PartitionSpec as P

ITERS = 3
AXES = ("space", "mem")


def product(a, b, axis):
    return lax.dot_general(
        a,
        b,
        (((1,), (axis,)), ((), ())),
        precision=lax.Precision.HIGHEST,
        preferred_element_type=jnp.float32,
    )


def half(array, which, axis):
    size = array.shape[axis] // 2
    return lax.dynamic_slice_in_dim(array, which * size, size, axis)


def per_device(prior_ensemble, terminal_particles, reverse_perturbation, measured_angles):
    space, mem = lax.axis_size("space"), lax.axis_size("mem")
    core = lax.rem(lax.axis_index("space"), 2)
    swap = [(i, i ^ 1) for i in range(space)]
    depth = 8
    width = mem // depth
    planes = [
        [s * mem + z * width + y for s in range(c, space, 2) for y in range(width)]
        for c in range(2)
        for z in range(depth)
    ]
    columns = [[z * width + y for z in range(depth)] for y in range(width)]
    peers = len(planes[0])

    def in_plane(blocks):
        return lax.all_to_all(
            blocks, AXES, split_axis=0, concat_axis=0, axis_index_groups=planes
        )

    def in_column(blocks):
        return lax.all_to_all(
            blocks, "mem", split_axis=0, concat_axis=0, axis_index_groups=columns
        )

    own = lax.all_to_all(prior_ensemble, "mem", split_axis=1, concat_axis=0, tiled=True)
    samples = jnp.concatenate([terminal_particles[None], reverse_perturbation[:-1]])
    other = lax.ppermute(half(samples, 1 - core, 1), "space", swap)
    samples = jnp.concatenate([half(samples, core, 1), other], axis=-1)
    angles = jnp.concatenate(
        [measured_angles, lax.ppermute(measured_angles, "space", swap)]
    )
    own, samples, angles = lax.optimization_barrier((own, samples, angles))
    particles, perturbation = samples[0], samples[1:]
    far_members = lax.ppermute(own, "space", swap)
    members = jnp.concatenate([own, far_members], axis=1)
    temper = math.sqrt(measured_angles.shape[0] * space * mem)
    lengths = jnp.sum(members * members, axis=1)

    z = particles
    count, total = z.shape[0], members.shape[0]
    rows = count // peers
    for step in range(ITERS):
        t = 1.0 - step / ITERS
        dt = 1.0 / ITERS
        alpha = 1.0 - 0.5 * t
        drift = -0.5 / alpha
        g2 = 1.0 + t / alpha
        damp = 1.0 - t
        gram = product(z, members, 1)
        partial = (2.0 * alpha * gram - alpha * alpha * lengths[None, :]) / (
            2.0 * t * temper
        )
        plane_sum = jnp.sum(in_plane(partial.reshape(peers, rows, total)), axis=0)
        spread = jnp.broadcast_to(plane_sum[None], (depth, rows, total))
        logits = jnp.sum(in_column(spread), axis=0)
        weights = jax.nn.softmax(logits, axis=1)
        weights = in_plane(jnp.broadcast_to(weights[None], (peers, rows, total)))
        pull = damp * 4.0 * (angles[None, :] - jnp.arctan(z)) / (1.0 + z * z)
        rest = z + dt * (-drift * z + g2 * (pull - z / t))
        weights = weights.reshape(count, total)
        if step == ITERS - 1:
            break
        blend = product(weights, members, 0)
        z = (
            rest
            + math.sqrt(dt * g2) * perturbation[step]
            + (dt * g2 * alpha / t) * blend
        )
    mine = measured_angles.shape[0]
    scale = dt * g2 * alpha / t
    far = rest[:, mine:] + scale * product(weights, far_members, 0)
    back = lax.ppermute(far, "space", swap)
    kept = rest[:, :mine] + scale * product(weights, own, 0)
    first = core == 0
    return (
        jnp.concatenate(
            [jnp.where(first, kept, back), jnp.where(first, back, kept)], axis=0
        )
        + math.sqrt(dt * g2) * reverse_perturbation[-1]
    )


def solution(mesh):
    in_specs = (
        P("mem", "space"),
        P(None, ("space", "mem")),
        P(None, None, ("space", "mem")),
        P(("space", "mem")),
    )
    out_specs = P(None, ("space", "mem"))
    return jax.shard_map(
        per_device, mesh=mesh, in_specs=in_specs, out_specs=out_specs, check_vma=False
    )
```

```python
import functools
import math

import jax
import jax.numpy as jnp
from jax import lax
from jax.experimental import pallas as pl
from jax.experimental.pallas import tpu as pltpu
from jax.sharding import PartitionSpec as P

ITERS = 3
DEPTH = 8
AXES = ("space", "mem")
VMEM = pl.BlockSpec(memory_space=pltpu.VMEM)
SMEM = pl.BlockSpec(memory_space=pltpu.SMEM)


def constants(step):
    t = 1.0 - step / ITERS
    dt = 1.0 / ITERS
    alpha = 1.0 - 0.5 * t
    drift = -0.5 / alpha
    g2 = 1.0 + t / alpha
    damp = 1.0 - t
    keep = 1.0 - dt * drift - dt * g2 / t
    gain = dt * g2 * alpha / t
    pull = dt * g2 * damp * 4.0
    noise = math.sqrt(dt * g2)
    return alpha, t, keep, gain, pull, noise


A0, T0, KEEP0, GAIN0, PULL0, NOISE0 = constants(0)
A1, T1, KEEP1, GAIN1, PULL1, NOISE1 = constants(1)
A2, T2, KEEP2, GAIN2, PULL2, NOISE2 = constants(2)


def product(a, b, axis):
    return lax.dot_general(
        a,
        b,
        (((1,), (axis,)), ((), ())),
        precision=lax.Precision.HIGHEST,
        preferred_element_type=jnp.float32,
    )


def misfit(z, angles):
    x = jnp.abs(z)
    square = 1.0 + z * z
    far = x > 2.414213562373095
    mid = x > 0.4142135623730951
    num = jnp.where(far, -1.0, jnp.where(mid, x - 1.0, x))
    den = jnp.where(far, x, jnp.where(mid, x + 1.0, 1.0))
    base = jnp.where(far, math.pi / 2, jnp.where(mid, math.pi / 4, 0.0))
    r = 1.0 / (den * square)
    q = num * square * r
    s = q * q
    p = 8.05374449538e-2 * s - 1.38776856032e-1
    p = (p * s + 1.99777106478e-1) * s - 3.33329491539e-1
    y = base + (p * s * q + q)
    return (angles - jnp.where(z < 0.0, -y, y)) * (den * r)


def softmax(raw, scale):
    logits = raw * (1.0 / scale)
    e = jnp.exp(logits - jnp.max(logits, axis=1, keepdims=True))
    return e / jnp.sum(e, axis=1, keepdims=True)


def tree_sum(terms):
    while len(terms) > 1:
        terms = [a + b for a, b in zip(terms[::2], terms[1::2])]
    return terms[0]


def first_kernel(core, own, far, z, lengths, members, out):
    width = own.shape[1]
    peers, rows = out.shape[0], out.shape[1] // 2
    count = peers * rows
    members[:, :width] = own[...]
    members[:, width:] = far[...]
    half = members[pl.ds(pl.multiple_of(core[0] * count, count), count), :]
    gram = product(jnp.concatenate([z[...], half]), members[...], 1)
    raw = 2.0 * A0 * gram[:count] - A0 * A0 * lengths[...]
    out[:, :rows, :] = raw.reshape(peers, rows, -1)
    out[:, rows:, :] = gram[count:].reshape(peers, rows, -1)


def spread_kernel(got, out):
    total = tree_sum([got[i] for i in range(got.shape[0])])
    for i in range(out.shape[0]):
        out[i] = total


def weigh_kernel(scale, got, out):
    total = tree_sum([got[i] for i in range(got.shape[0])])
    rows = out.shape[1] // 2
    weights = softmax(total[:rows], scale)
    for i in range(out.shape[0]):
        out[i, :rows, :] = weights
        out[i, rows:, :] = total[rows:]


def step_kernel(got, members, u, noise, angles, lengths, out, y_out, pairs):
    peers, rows = out.shape[0], out.shape[1] // 2
    count = peers * rows
    pairs[...] = got[:, rows:, :].reshape(count, -1)
    blend = product(got[:, :rows, :].reshape(count, -1), members[...], 0)
    z = u[...] + GAIN0 * blend
    y = KEEP1 * z + PULL1 * misfit(z, angles[...]) + NOISE1 * noise[...]
    y_out[...] = y
    gram = product(jnp.concatenate([z, y]), members[...], 1)
    raw1 = 2.0 * A1 * gram[:count] - A1 * A1 * lengths[...]
    raw2 = 2.0 * A2 * gram[count:] - A2 * A2 * lengths[...]
    out[:, :rows, :] = raw1.reshape(peers, rows, -1)
    out[:, rows:, :] = raw2.reshape(peers, rows, -1)


def weigh_twice_kernel(scale1, scale2, core, got, near, far, out):
    total = tree_sum([got[i] for i in range(got.shape[0])])
    rows = out.shape[1] // 2
    w1 = softmax(total[:rows], scale1)
    width = near.shape[0]
    low, high = w1[:, :width], w1[:, width:]
    first = core[0] == 0
    w1_pairs = product(jnp.where(first, low, high), near[...], 0) + product(
        jnp.where(first, high, low), far[...], 0
    )
    w2 = softmax(total[rows:] + (2.0 * A2 * GAIN1) * w1_pairs, scale2)
    for i in range(out.shape[0]):
        out[i, :rows, :] = w1
        out[i, rows:, :] = w2


def last_kernel(got, members, y, angles, kept, sent):
    peers, rows = got.shape[0], got.shape[1] // 2
    count = peers * rows
    weights = jnp.concatenate(
        [
            got[:, :rows, :].reshape(count, -1),
            got[:, rows:, :].reshape(count, -1),
        ]
    )
    blend = product(weights, members[...], 0)
    z = y[...] + GAIN1 * blend[:count]
    z = KEEP2 * z + PULL2 * misfit(z, angles[...]) + GAIN2 * blend[count:]
    width = kept.shape[1]
    kept[...] = z[:, :width]
    sent[...] = z[:, width:]


def call(kernel, name, outs, *args):
    shapes = tuple(jax.ShapeDtypeStruct(s, jnp.float32) for s in outs)
    specs = [SMEM if a.dtype == jnp.int32 else VMEM for a in args]
    result = pl.pallas_call(
        kernel,
        out_shape=shapes,
        in_specs=specs,
        out_specs=tuple(VMEM for _ in outs),
        compiler_params=pltpu.CompilerParams(vmem_limit_bytes=24 << 20),
        name=name,
    )(*args)
    return result if len(outs) > 1 else result[0]


def half(array, which, axis):
    size = array.shape[axis] // 2
    return lax.dynamic_slice_in_dim(array, which * size, size, axis)


def per_device(prior_ensemble, terminal_particles, reverse_perturbation, measured_angles):
    space, mem = lax.axis_size("space"), lax.axis_size("mem")
    core = lax.rem(lax.axis_index("space"), 2)
    core_ref = core.astype(jnp.int32).reshape(1)
    swap = [(i, i ^ 1) for i in range(space)]
    span = mem // DEPTH
    planes = [
        [s * mem + z * span + y for s in range(c, space, 2) for y in range(span)]
        for c in range(2)
        for z in range(DEPTH)
    ]
    columns = [[z * span + y for z in range(DEPTH)] for y in range(span)]
    peers = len(planes[0])

    def other_core(array):
        return lax.ppermute(array, "space", swap)

    def in_plane(blocks):
        return lax.all_to_all(
            blocks, AXES, split_axis=0, concat_axis=0, axis_index_groups=planes
        )

    def in_column(blocks):
        return lax.all_to_all(
            blocks, "mem", split_axis=0, concat_axis=0, axis_index_groups=columns
        )

    temper = math.sqrt(measured_angles.shape[0] * space * mem)
    own = lax.all_to_all(prior_ensemble, "mem", split_axis=1, concat_axis=0, tiled=True)
    samples = jnp.concatenate([terminal_particles[None], reverse_perturbation[:-1]])
    other = other_core(half(samples, 1 - core, 1))
    samples = jnp.concatenate([half(samples, core, 1), other], axis=-1)
    angles = jnp.concatenate([measured_angles, other_core(measured_angles)])[None, :]
    z0 = samples[0]
    u0 = KEEP0 * z0 + PULL0 * misfit(z0, angles) + NOISE0 * samples[1]
    own, z0, u0, e1, angles = lax.optimization_barrier(
        (own, z0, u0, samples[2], angles)
    )
    far = other_core(own)
    lengths = (jnp.sum(own * own, axis=1) + jnp.sum(far * far, axis=1))[None, :]
    total, width = own.shape
    count = z0.shape[0]
    rows = count // peers
    wide = (peers, 2 * rows, total)
    deep = (DEPTH, 2 * rows, total)

    members, blocks = call(
        first_kernel, "first", [(total, 2 * width), wide], core_ref, own, far, z0, lengths
    )
    blocks = call(spread_kernel, "spread", [deep], in_plane(blocks))
    weigh = functools.partial(weigh_kernel, 2.0 * T0 * temper)
    blocks = call(weigh, "weigh", [wide], in_column(blocks))
    blocks, y, near = call(
        step_kernel,
        "step",
        [wide, z0.shape, (count, total)],
        in_plane(blocks),
        members,
        u0,
        e1,
        angles,
        lengths,
    )
    pairs_far = other_core(near)
    blocks = call(spread_kernel, "spread", [deep], in_plane(blocks))
    weigh = functools.partial(weigh_twice_kernel, 2.0 * T1 * temper, 2.0 * T2 * temper)
    blocks = call(
        weigh, "weigh_twice", [wide], core_ref, in_column(blocks), near, pairs_far
    )
    kept, sent = call(
        last_kernel,
        "last",
        [(count, width), (count, width)],
        in_plane(blocks),
        members,
        y,
        angles,
    )
    back = other_core(sent)
    first = core == 0
    return (
        jnp.concatenate(
            [jnp.where(first, kept, back), jnp.where(first, back, kept)], axis=0
        )
        + NOISE2 * reverse_perturbation[-1]
    )


def solution(mesh):
    in_specs = (
        P("mem", "space"),
        P(None, ("space", "mem")),
        P(None, None, ("space", "mem")),
        P(("space", "mem")),
    )
    out_specs = P(None, ("space", "mem"))
    return jax.shard_map(
        per_device, mesh=mesh, in_specs=in_specs, out_specs=out_specs, check_vma=False
    )
```

```python
import functools
import math

import jax
import jax.numpy as jnp
from jax import lax
from jax.experimental import pallas as pl
from jax.experimental.pallas import tpu as pltpu
from jax.sharding import PartitionSpec as P

ITERS = 3
DEPTH = 8
AXES = ("space", "mem")
VMEM = pl.BlockSpec(memory_space=pltpu.VMEM)
SMEM = pl.BlockSpec(memory_space=pltpu.SMEM)
ANY = pl.BlockSpec(memory_space=pl.ANY)
DMA = pltpu.SemaphoreType.DMA


def constants(step):
    t = 1.0 - step / ITERS
    dt = 1.0 / ITERS
    alpha = 1.0 - 0.5 * t
    drift = -0.5 / alpha
    g2 = 1.0 + t / alpha
    damp = 1.0 - t
    keep = 1.0 - dt * drift - dt * g2 / t
    gain = dt * g2 * alpha / t
    pull = dt * g2 * damp * 4.0
    noise = math.sqrt(dt * g2)
    return alpha, t, keep, gain, pull, noise


A0, T0, KEEP0, GAIN0, PULL0, NOISE0 = constants(0)
A1, T1, KEEP1, GAIN1, PULL1, NOISE1 = constants(1)
A2, T2, KEEP2, GAIN2, PULL2, NOISE2 = constants(2)


def product(a, b, axis):
    return lax.dot_general(
        a,
        b,
        (((1,), (axis,)), ((), ())),
        precision=lax.Precision.HIGHEST,
        preferred_element_type=jnp.float32,
    )


def misfit(z, angles):
    x = jnp.abs(z)
    square = 1.0 + z * z
    far = x > 2.414213562373095
    mid = x > 0.4142135623730951
    num = jnp.where(far, -1.0, jnp.where(mid, x - 1.0, x))
    den = jnp.where(far, x, jnp.where(mid, x + 1.0, 1.0))
    base = jnp.where(far, math.pi / 2, jnp.where(mid, math.pi / 4, 0.0))
    r = 1.0 / (den * square)
    q = num * square * r
    s = q * q
    p = 8.05374449538e-2 * s - 1.38776856032e-1
    p = (p * s + 1.99777106478e-1) * s - 3.33329491539e-1
    y = base + (p * s * q + q)
    return (angles - jnp.where(z < 0.0, -y, y)) * (den * r)


def softmax(raw, scale):
    logits = raw * (1.0 / scale)
    e = jnp.exp(logits - jnp.max(logits, axis=1, keepdims=True))
    return e / jnp.sum(e, axis=1, keepdims=True)


def tree_sum(terms):
    while len(terms) > 1:
        terms = [a + b for a, b in zip(terms[::2], terms[1::2])]
    return terms[0]


def first_kernel(core, own, far, z, lengths, members, out):
    width = own.shape[1]
    peers, rows = out.shape[0], out.shape[1] // 2
    count = peers * rows
    members[:, :width] = own[...]
    members[:, width:] = far[...]
    half = members[pl.ds(pl.multiple_of(core[0] * count, count), count), :]
    gram = product(jnp.concatenate([z[...], half]), members[...], 1)
    raw = 2.0 * A0 * gram[:count] - A0 * A0 * lengths[...]
    out[:, :rows, :] = raw.reshape(peers, rows, -1)
    out[:, rows:, :] = gram[count:].reshape(peers, rows, -1)


def spread_kernel(got, out):
    total = tree_sum([got[i] for i in range(got.shape[0])])
    for i in range(out.shape[0]):
        out[i] = total


def weigh_kernel(scale, got, out):
    total = tree_sum([got[i] for i in range(got.shape[0])])
    rows = out.shape[1] // 2
    weights = softmax(total[:rows], scale)
    for i in range(out.shape[0]):
        out[i, :rows, :] = weights
        out[i, rows:, :] = total[rows:]


def step_kernel(
    got, members, u, noise, angles, lengths, out, y_out, pairs, y_ref, y_sem, pairs_sem
):
    peers, rows = out.shape[0], out.shape[1] // 2
    count = peers * rows
    pairs_copy = pltpu.make_async_copy(got.at[:, pl.ds(rows, rows), :], pairs, pairs_sem)
    pairs_copy.start()
    blend = product(got[:, :rows, :].reshape(count, -1), members[...], 0)
    z = u[...] + GAIN0 * blend
    y = KEEP1 * z + PULL1 * misfit(z, angles[...]) + NOISE1 * noise[...]
    y_ref[...] = y
    y_copy = pltpu.make_async_copy(y_ref, y_out, y_sem)
    y_copy.start()
    gram = product(jnp.concatenate([z, y]), members[...], 1)
    raw1 = 2.0 * A1 * gram[:count] - A1 * A1 * lengths[...]
    raw2 = 2.0 * A2 * gram[count:] - A2 * A2 * lengths[...]
    out[:, :rows, :] = raw1.reshape(peers, rows, -1)
    out[:, rows:, :] = raw2.reshape(peers, rows, -1)
    pairs_copy.wait()
    y_copy.wait()


def weigh_twice_kernel(
    scale1, scale2, core, got, near_in, far_in, out, near, far, near_sem, far_sem
):
    near_copy = pltpu.make_async_copy(near_in, near, near_sem)
    far_copy = pltpu.make_async_copy(far_in, far, far_sem)
    near_copy.start()
    far_copy.start()
    total = tree_sum([got[i] for i in range(got.shape[0])])
    rows = out.shape[1] // 2
    w1 = softmax(total[:rows], scale1)
    for i in range(out.shape[0]):
        out[i, :rows, :] = w1
    width = near.shape[0]
    low, high = w1[:, :width], w1[:, width:]
    first = core[0] == 0
    near_copy.wait()
    w1_pairs = product(jnp.where(first, low, high), near[...], 0)
    far_copy.wait()
    w1_pairs += product(jnp.where(first, high, low), far[...], 0)
    w2 = softmax(total[rows:] + (2.0 * A2 * GAIN1) * w1_pairs, scale2)
    for i in range(out.shape[0]):
        out[i, rows:, :] = w2


def last_kernel(first_lane, got, members, y, noise, angles, out):
    peers, rows = got.shape[0], got.shape[1] // 2
    count = peers * rows
    lanes = pl.ds(first_lane, out.shape[1])
    weights = jnp.concatenate(
        [
            got[:, :rows, :].reshape(count, -1),
            got[:, rows:, :].reshape(count, -1),
        ]
    )
    blend = product(weights, members[:, lanes], 0)
    z = y[:, lanes] + GAIN1 * blend[:count]
    z = KEEP2 * z + PULL2 * misfit(z, angles[:, lanes]) + GAIN2 * blend[count:]
    out[...] = z + NOISE2 * noise[:, lanes]


def place_kernel(core, kept, back, out):
    count = kept.shape[0]
    out[pl.ds(pl.multiple_of(core[0] * count, count), count), :] = kept[...]
    out[pl.ds(pl.multiple_of((1 - core[0]) * count, count), count), :] = back[...]


def cut_kernel(array, out, sems):
    width = out.shape[2]
    copies = [
        pltpu.make_async_copy(
            array.at[:, pl.ds(i * width, width)], out.at[i], sems.at[i]
        )
        for i in range(out.shape[0])
    ]
    for copy in copies:
        copy.start()
    for copy in copies:
        copy.wait()


def call(kernel, name, outs, *args, products=1, anywhere=(), scratch=()):
    shapes = tuple(jax.ShapeDtypeStruct(s, jnp.float32) for s in outs)
    result = pl.pallas_call(
        kernel,
        out_shape=shapes,
        in_specs=[
            SMEM if a.dtype == jnp.int32 else ANY if i in anywhere else VMEM
            for i, a in enumerate(args)
        ],
        out_specs=tuple(
            ANY if len(args) + i in anywhere else VMEM for i in range(len(outs))
        ),
        scratch_shapes=list(scratch),
        compiler_params=pltpu.CompilerParams(vmem_limit_bytes=24 << 20),
        cost_estimate=pl.CostEstimate(
            flops=12 * 256 * 512 * 512 * products,
            bytes_accessed=sum(4 * math.prod(s) for s in outs),
            transcendentals=0,
        ),
        name=name,
    )(*args)
    return result if len(outs) > 1 else result[0]


def half(array, which, axis):
    size = array.shape[axis] // 2
    return lax.dynamic_slice_in_dim(array, which * size, size, axis)


def per_device(prior_ensemble, terminal_particles, reverse_perturbation, measured_angles):
    space, mem = lax.axis_size("space"), lax.axis_size("mem")
    core = lax.rem(lax.axis_index("space"), 2)
    core_ref = core.astype(jnp.int32).reshape(1)
    swap = [(i, i ^ 1) for i in range(space)]
    span = mem // DEPTH
    planes = [
        [s * mem + z * span + y for s in range(c, space, 2) for y in range(span)]
        for c in range(2)
        for z in range(DEPTH)
    ]
    columns = [[z * span + y for z in range(DEPTH)] for y in range(span)]
    peers = len(planes[0])

    def other_core(array):
        return lax.ppermute(array, "space", swap)

    def in_plane(blocks):
        return lax.all_to_all(
            blocks, AXES, split_axis=0, concat_axis=0, axis_index_groups=planes
        )

    def in_column(blocks):
        return lax.all_to_all(
            blocks, "mem", split_axis=0, concat_axis=0, axis_index_groups=columns
        )

    temper = math.sqrt(measured_angles.shape[0] * space * mem)
    width = measured_angles.shape[0]
    cut = call(
        cut_kernel,
        "cut",
        [(mem, prior_ensemble.shape[0], width)],
        prior_ensemble,
        anywhere=(0, 1),
        scratch=[DMA((mem,))],
    )
    own = lax.all_to_all(cut, "mem", split_axis=0, concat_axis=0)
    own = own.reshape(mem * prior_ensemble.shape[0], width)
    def pair_up(arrays):
        other = other_core(half(arrays, 1 - core, 1))
        return jnp.concatenate([half(arrays, core, 1), other], axis=-1)

    e1, e2 = pair_up(reverse_perturbation[1:])
    z0, e0 = pair_up(
        jnp.concatenate([terminal_particles[None], reverse_perturbation[:1]])
    )
    angles = jnp.concatenate([measured_angles, other_core(measured_angles)])[None, :]
    u0 = KEEP0 * z0 + PULL0 * misfit(z0, angles) + NOISE0 * e0
    own, z0, u0, e1, e2, angles = lax.optimization_barrier(
        (own, z0, u0, e1, e2, angles)
    )
    far = other_core(own)
    lengths = (jnp.sum(own * own, axis=1) + jnp.sum(far * far, axis=1))[None, :]
    total, width = own.shape
    count = z0.shape[0]
    rows = count // peers
    wide = (peers, 2 * rows, total)
    deep = (DEPTH, 2 * rows, total)

    members, blocks = call(
        first_kernel, "first", [(total, 2 * width), wide], core_ref, own, far, z0, lengths
    )
    blocks = call(spread_kernel, "spread", [deep], in_plane(blocks))
    weigh = functools.partial(weigh_kernel, 2.0 * T0 * temper)
    blocks = call(weigh, "weigh", [wide], in_column(blocks))
    blocks, y, near = call(
        step_kernel,
        "step",
        [wide, z0.shape, (peers, rows, total)],
        in_plane(blocks),
        members,
        u0,
        e1,
        angles,
        lengths,
        products=3,
        anywhere=(7, 8),
        scratch=[pltpu.VMEM(z0.shape, jnp.float32), DMA, DMA],
    )
    near = near.reshape(count, total)
    pairs_far = other_core(near)
    blocks = call(spread_kernel, "spread", [deep], in_plane(blocks))
    weigh = functools.partial(weigh_twice_kernel, 2.0 * T1 * temper, 2.0 * T2 * temper)
    half_pairs = pltpu.VMEM((count, total), jnp.float32)
    blocks = call(
        weigh,
        "weigh_twice",
        [wide],
        core_ref,
        in_column(blocks),
        near,
        pairs_far,
        anywhere=(2, 3),
        scratch=[half_pairs, half_pairs, DMA, DMA],
    )
    blocks = in_plane(blocks)
    last = functools.partial(last_kernel, width)
    sent = call(last, "last_far", [(count, width)], blocks, members, y, e2, angles)
    back = other_core(sent)
    last = functools.partial(last_kernel, 0)
    kept = call(last, "last_near", [(count, width)], blocks, members, y, e2, angles)
    return call(place_kernel, "place", [(2 * count, width)], core_ref, kept, back)


def solution(mesh):
    in_specs = (
        P("mem", "space"),
        P(None, ("space", "mem")),
        P(None, None, ("space", "mem")),
        P(("space", "mem")),
    )
    out_specs = P(None, ("space", "mem"))
    return jax.shard_map(
        per_device, mesh=mesh, in_specs=in_specs, out_specs=out_specs, check_vma=False
    )
```

```python
import functools
import math

import jax
import jax.numpy as jnp
from jax import lax
from jax.experimental import pallas as pl
from jax.experimental.pallas import tpu as pltpu
from jax.sharding import PartitionSpec as P

ITERS = 3
DEPTH = 8
AXES = ("space", "mem")
VMEM = pl.BlockSpec(memory_space=pltpu.VMEM)
SMEM = pl.BlockSpec(memory_space=pltpu.SMEM)
ANY = pl.BlockSpec(memory_space=pl.ANY)
DMA = pltpu.SemaphoreType.DMA


def constants(step):
    t = 1.0 - step / ITERS
    dt = 1.0 / ITERS
    alpha = 1.0 - 0.5 * t
    drift = -0.5 / alpha
    g2 = 1.0 + t / alpha
    damp = 1.0 - t
    keep = 1.0 - dt * drift - dt * g2 / t
    gain = dt * g2 * alpha / t
    pull = dt * g2 * damp * 4.0
    noise = math.sqrt(dt * g2)
    return alpha, t, keep, gain, pull, noise


A0, T0, KEEP0, GAIN0, PULL0, NOISE0 = constants(0)
A1, T1, KEEP1, GAIN1, PULL1, NOISE1 = constants(1)
A2, T2, KEEP2, GAIN2, PULL2, NOISE2 = constants(2)


def product(a, b, axis):
    return lax.dot_general(
        a,
        b,
        (((1,), (axis,)), ((), ())),
        precision=lax.Precision.HIGHEST,
        preferred_element_type=jnp.float32,
    )


def misfit(z, angles):
    x = jnp.abs(z)
    square = 1.0 + z * z
    far = x > 2.414213562373095
    mid = x > 0.4142135623730951
    num = jnp.where(far, -1.0, jnp.where(mid, x - 1.0, x))
    den = jnp.where(far, x, jnp.where(mid, x + 1.0, 1.0))
    base = jnp.where(far, math.pi / 2, jnp.where(mid, math.pi / 4, 0.0))
    r = 1.0 / (den * square)
    q = num * square * r
    s = q * q
    p = 8.05374449538e-2 * s - 1.38776856032e-1
    p = (p * s + 1.99777106478e-1) * s - 3.33329491539e-1
    y = base + (p * s * q + q)
    return (angles - jnp.where(z < 0.0, -y, y)) * (den * r)


def softmax(raw, scale):
    logits = raw * (1.0 / scale)
    e = jnp.exp(logits - jnp.max(logits, axis=1, keepdims=True))
    return e / jnp.sum(e, axis=1, keepdims=True)


def tree_sum(terms):
    while len(terms) > 1:
        terms = [a + b for a, b in zip(terms[::2], terms[1::2])]
    return terms[0]


def pack_pairs(first, gram):
    rows = gram.shape[0] // 2
    low, high = gram[:rows], gram[rows:]

    def blocks(array, start):
        wrapped = jnp.concatenate([array, array], axis=1)
        return wrapped[:, start * rows : (start + 3) * rows]

    low = jnp.where(first, blocks(low, 0), blocks(low, 2))
    high = jnp.where(first, blocks(high, 1), blocks(high, 3))
    return jnp.concatenate([low, high])


def times_pairs(first, w, near, far):
    rows = near.shape[0] // 2
    low, high = w[:, : 2 * rows], w[:, 2 * rows :]
    w = jnp.where(first, w, jnp.concatenate([high, low], axis=1))
    parts = [w[:, i * rows : (i + 1) * rows] for i in range(4)]
    packed = [near[:rows], near[rows:], far[:rows], far[rows:]]
    sums = [product(parts[(i + 1) % 4], packed[i][:, rows : 2 * rows], 1) for i in range(4)]
    for i in range(4):
        ahead = product(parts[i], packed[i], 0)
        for k in range(3):
            sums[(i + k) % 4] += ahead[:, k * rows : (k + 1) * rows]
    low = jnp.concatenate(sums[:2], axis=1)
    high = jnp.concatenate(sums[2:], axis=1)
    return jnp.concatenate(
        [jnp.where(first, low, high), jnp.where(first, high, low)], axis=1
    )


def my_members(core, members):
    count = members.shape[0] // 2
    return members[pl.ds(pl.multiple_of(core[0] * count, count), count), :]


def own_kernel(core, own, z, out):
    stack = jnp.concatenate([z[:, : own.shape[1]], my_members(core, own)])
    out[...] = product(stack, own[...], 1)


def first_kernel(core, own, far, z, lengths, gram_own, members, out):
    width = own.shape[1]
    total = own.shape[0]
    peers, rows = out.shape[0], out.shape[1]
    count = peers * rows
    members[:, :width] = own[...]
    members[:, width:] = far[...]
    stack = jnp.concatenate([z[:, width:], my_members(core, far)])
    gram = gram_own[...] + product(stack, far[...], 1)
    raw = 2.0 * A0 * gram[:count] - A0 * A0 * lengths[...]
    out[:, :, :total] = raw.reshape(peers, rows, -1)
    pairs = pack_pairs(core[0] == 0, gram[count:])
    out[:, :, total:] = pairs.reshape(peers, rows, -1)


def spread_kernel(got, out):
    total = tree_sum([got[i] for i in range(got.shape[0])])
    for i in range(out.shape[0]):
        out[i] = total


def weigh_kernel(scale, members, got, out):
    total = tree_sum([got[i] for i in range(got.shape[0])])
    weights = softmax(total[:, :members], scale)
    for i in range(out.shape[0]):
        out[i, :, :members] = weights
        out[i, :, members:] = total[:, members:]


def step_kernel(
    got, members, u, noise, angles, lengths, out, y_out, pairs, y_ref, y_sem, pairs_sem
):
    peers, rows = out.shape[0], out.shape[1] // 2
    count = peers * rows
    total, packed = members.shape[0], pairs.shape[2]
    pairs_copy = pltpu.make_async_copy(
        got.at[:, :, pl.ds(total, packed)], pairs, pairs_sem
    )
    pairs_copy.start()
    blend = product(got[:, :, :total].reshape(count, -1), members[...], 0)
    z = u[...] + GAIN0 * blend
    y = KEEP1 * z + PULL1 * misfit(z, angles[...]) + NOISE1 * noise[...]
    y_ref[...] = y
    y_copy = pltpu.make_async_copy(y_ref, y_out, y_sem)
    y_copy.start()
    gram = product(jnp.concatenate([z, y]), members[...], 1)
    raw1 = 2.0 * A1 * gram[:count] - A1 * A1 * lengths[...]
    raw2 = 2.0 * A2 * gram[count:] - A2 * A2 * lengths[...]
    out[:, :rows, :] = raw1.reshape(peers, rows, -1)
    out[:, rows:, :] = raw2.reshape(peers, rows, -1)
    pairs_copy.wait()
    y_copy.wait()


def weigh_twice_kernel(
    scale1, scale2, core, got, near_in, far_in, out, near, far, near_sem, far_sem
):
    near_copy = pltpu.make_async_copy(near_in, near, near_sem)
    far_copy = pltpu.make_async_copy(far_in, far, far_sem)
    near_copy.start()
    far_copy.start()
    total = tree_sum([got[i] for i in range(got.shape[0])])
    rows = out.shape[1] // 2
    w1 = softmax(total[:rows], scale1)
    for i in range(out.shape[0]):
        out[i, :rows, :] = w1
    near_copy.wait()
    far_copy.wait()
    w1_pairs = times_pairs(core[0] == 0, w1, near[...], far[...])
    w2 = softmax(total[rows:] + (2.0 * A2 * GAIN1) * w1_pairs, scale2)
    for i in range(out.shape[0]):
        out[i, rows:, :] = w2


def last_kernel(first_lane, got, members, y, noise, angles, out):
    peers, rows = got.shape[0], got.shape[1] // 2
    count = peers * rows
    lanes = pl.ds(first_lane, out.shape[1])
    weights = jnp.concatenate(
        [
            got[:, :rows, :].reshape(count, -1),
            got[:, rows:, :].reshape(count, -1),
        ]
    )
    blend = product(weights, members[:, lanes], 0)
    z = y[:, lanes] + GAIN1 * blend[:count]
    z = KEEP2 * z + PULL2 * misfit(z, angles[:, lanes]) + GAIN2 * blend[count:]
    out[...] = z + NOISE2 * noise[:, lanes]


def place_kernel(core, kept, back, out):
    count = kept.shape[0]
    out[pl.ds(pl.multiple_of(core[0] * count, count), count), :] = kept[...]
    out[pl.ds(pl.multiple_of((1 - core[0]) * count, count), count), :] = back[...]


def cut_kernel(array, out, sems):
    width = out.shape[2]
    copies = [
        pltpu.make_async_copy(
            array.at[:, pl.ds(i * width, width)], out.at[i], sems.at[i]
        )
        for i in range(out.shape[0])
    ]
    for copy in copies:
        copy.start()
    for copy in copies:
        copy.wait()


def call(kernel, name, outs, *args, products=1, anywhere=(), scratch=()):
    shapes = tuple(jax.ShapeDtypeStruct(s, jnp.float32) for s in outs)
    result = pl.pallas_call(
        kernel,
        out_shape=shapes,
        in_specs=[
            SMEM if a.dtype == jnp.int32 else ANY if i in anywhere else VMEM
            for i, a in enumerate(args)
        ],
        out_specs=tuple(
            ANY if len(args) + i in anywhere else VMEM for i in range(len(outs))
        ),
        scratch_shapes=list(scratch),
        compiler_params=pltpu.CompilerParams(vmem_limit_bytes=24 << 20),
        cost_estimate=pl.CostEstimate(
            flops=12 * 256 * 512 * 512 * products,
            bytes_accessed=sum(4 * math.prod(s) for s in outs),
            transcendentals=0,
        ),
        name=name,
    )(*args)
    return result if len(outs) > 1 else result[0]


def half(array, which, axis):
    size = array.shape[axis] // 2
    return lax.dynamic_slice_in_dim(array, which * size, size, axis)


def per_device(prior_ensemble, terminal_particles, reverse_perturbation, measured_angles):
    space, mem = lax.axis_size("space"), lax.axis_size("mem")
    core = lax.rem(lax.axis_index("space"), 2)
    core_ref = core.astype(jnp.int32).reshape(1)
    swap = [(i, i ^ 1) for i in range(space)]
    span = mem // DEPTH
    planes = [
        [s * mem + z * span + y for s in range(c, space, 2) for y in range(span)]
        for c in range(2)
        for z in range(DEPTH)
    ]
    columns = [[z * span + y for z in range(DEPTH)] for y in range(span)]
    peers = len(planes[0])

    def other_core(array):
        return lax.ppermute(array, "space", swap)

    def in_plane(blocks):
        return lax.all_to_all(
            blocks, AXES, split_axis=0, concat_axis=0, axis_index_groups=planes
        )

    def in_column(blocks):
        return lax.all_to_all(
            blocks, "mem", split_axis=0, concat_axis=0, axis_index_groups=columns
        )

    temper = math.sqrt(measured_angles.shape[0] * space * mem)
    width = measured_angles.shape[0]
    cut = call(
        cut_kernel,
        "cut",
        [(mem, prior_ensemble.shape[0], width)],
        prior_ensemble,
        anywhere=(0, 1),
        scratch=[DMA((mem,))],
    )
    own = lax.all_to_all(cut, "mem", split_axis=0, concat_axis=0)
    own = own.reshape(mem * prior_ensemble.shape[0], width)
    def pair_up(arrays):
        other = other_core(half(arrays, 1 - core, 1))
        return jnp.concatenate([half(arrays, core, 1), other], axis=-1)

    e1, e2 = pair_up(reverse_perturbation[1:])
    z0, e0 = pair_up(
        jnp.concatenate([terminal_particles[None], reverse_perturbation[:1]])
    )
    angles = jnp.concatenate([measured_angles, other_core(measured_angles)])[None, :]
    u0 = KEEP0 * z0 + PULL0 * misfit(z0, angles) + NOISE0 * e0
    own, z0, u0, e1, e2, angles = lax.optimization_barrier(
        (own, z0, u0, e1, e2, angles)
    )
    far = other_core(own)
    lengths = (jnp.sum(own * own, axis=1) + jnp.sum(far * far, axis=1))[None, :]
    total, width = own.shape
    count = z0.shape[0]
    rows = count // peers
    packed = 3 * total // 4
    wide = (peers, 2 * rows, total)
    deep = (DEPTH, 2 * rows, total)

    gram_own = call(own_kernel, "own", [(2 * count, total)], core_ref, own, z0)
    members, blocks = call(
        first_kernel,
        "first",
        [(total, 2 * width), (peers, rows, total + packed)],
        core_ref,
        own,
        far,
        z0,
        lengths,
        gram_own,
    )
    blocks = call(
        spread_kernel, "spread", [(DEPTH, rows, total + packed)], in_plane(blocks)
    )
    weigh = functools.partial(weigh_kernel, 2.0 * T0 * temper, total)
    blocks = call(weigh, "weigh", [(peers, rows, total + packed)], in_column(blocks))
    blocks, y, near = call(
        step_kernel,
        "step",
        [wide, z0.shape, (peers, rows, packed)],
        in_plane(blocks),
        members,
        u0,
        e1,
        angles,
        lengths,
        products=3,
        anywhere=(7, 8),
        scratch=[pltpu.VMEM(z0.shape, jnp.float32), DMA, DMA],
    )
    near = near.reshape(count, packed)
    pairs_far = other_core(near)
    blocks = call(spread_kernel, "spread", [deep], in_plane(blocks))
    weigh = functools.partial(weigh_twice_kernel, 2.0 * T1 * temper, 2.0 * T2 * temper)
    half_pairs = pltpu.VMEM((count, packed), jnp.float32)
    blocks = call(
        weigh,
        "weigh_twice",
        [wide],
        core_ref,
        in_column(blocks),
        near,
        pairs_far,
        anywhere=(2, 3),
        scratch=[half_pairs, half_pairs, DMA, DMA],
    )
    blocks = in_plane(blocks)
    last = functools.partial(last_kernel, width)
    sent = call(last, "last_far", [(count, width)], blocks, members, y, e2, angles)
    back = other_core(sent)
    last = functools.partial(last_kernel, 0)
    kept = call(last, "last_near", [(count, width)], blocks, members, y, e2, angles)
    return call(place_kernel, "place", [(2 * count, width)], core_ref, kept, back)


def solution(mesh):
    in_specs = (
        P("mem", "space"),
        P(None, ("space", "mem")),
        P(None, None, ("space", "mem")),
        P(("space", "mem")),
    )
    out_specs = P(None, ("space", "mem"))
    return jax.shard_map(
        per_device, mesh=mesh, in_specs=in_specs, out_specs=out_specs, check_vma=False
    )
```

```python
import functools
import math

import jax
import jax.numpy as jnp
from jax import lax
from jax.experimental import pallas as pl
from jax.experimental.pallas import tpu as pltpu
from jax.sharding import PartitionSpec as P

ITERS = 3
DEPTH = 8
AXES = ("space", "mem")
VMEM = pl.BlockSpec(memory_space=pltpu.VMEM)
SMEM = pl.BlockSpec(memory_space=pltpu.SMEM)
ANY = pl.BlockSpec(memory_space=pl.ANY)
DMA = pltpu.SemaphoreType.DMA


def constants(step):
    t = 1.0 - step / ITERS
    dt = 1.0 / ITERS
    alpha = 1.0 - 0.5 * t
    drift = -0.5 / alpha
    g2 = 1.0 + t / alpha
    damp = 1.0 - t
    keep = 1.0 - dt * drift - dt * g2 / t
    gain = dt * g2 * alpha / t
    pull = dt * g2 * damp * 4.0
    noise = math.sqrt(dt * g2)
    return alpha, t, keep, gain, pull, noise


A0, T0, KEEP0, GAIN0, PULL0, NOISE0 = constants(0)
A1, T1, KEEP1, GAIN1, PULL1, NOISE1 = constants(1)
A2, T2, KEEP2, GAIN2, PULL2, NOISE2 = constants(2)


def product(a, b, axis):
    return lax.dot_general(
        a,
        b,
        (((1,), (axis,)), ((), ())),
        precision=lax.Precision.HIGHEST,
        preferred_element_type=jnp.float32,
    )


def misfit(z, angles):
    x = jnp.abs(z)
    square = 1.0 + z * z
    far = x > 2.414213562373095
    mid = x > 0.4142135623730951
    num = jnp.where(far, -1.0, jnp.where(mid, x - 1.0, x))
    den = jnp.where(far, x, jnp.where(mid, x + 1.0, 1.0))
    base = jnp.where(far, math.pi / 2, jnp.where(mid, math.pi / 4, 0.0))
    r = 1.0 / (den * square)
    q = num * square * r
    s = q * q
    p = 8.05374449538e-2 * s - 1.38776856032e-1
    p = (p * s + 1.99777106478e-1) * s - 3.33329491539e-1
    y = base + (p * s * q + q)
    return (angles - jnp.where(z < 0.0, -y, y)) * (den * r)


def softmax(raw, scale):
    logits = raw * (1.0 / scale)
    e = jnp.exp(logits - jnp.max(logits, axis=1, keepdims=True))
    return e / jnp.sum(e, axis=1, keepdims=True)


def tree_sum(terms):
    while len(terms) > 1:
        terms = [a + b for a, b in zip(terms[::2], terms[1::2])]
    return terms[0]


def pack_pairs(first, gram):
    size = gram.shape[0] // 2

    def block(row, column, other):
        rows = gram[row * size : (row + 1) * size]
        return jnp.where(
            first,
            rows[:, column * size : (column + 1) * size],
            rows[:, other * size : (other + 1) * size],
        )

    return jnp.concatenate(
        [block(0, 0, 2), block(0, 1, 3), block(1, 1, 3), block(0, 2, 1), block(1, 3, 0)],
        axis=1,
    )


def thirds(array):
    high = array.astype(jnp.bfloat16)
    rest = array - high.astype(jnp.float32)
    mid = rest.astype(jnp.bfloat16)
    return high, mid, (rest - mid.astype(jnp.float32)).astype(jnp.bfloat16)


def times_pairs(first, w, near, far):
    size, rows = near.shape[0], w.shape[0]
    w_high, w_mid, w_low = thirds(w)
    stacks = (
        jnp.concatenate([w_high, w_mid, w_low]),
        jnp.concatenate([w_high, w_mid]),
        w_high,
    )
    halves = jnp.where(first, near, far), jnp.where(first, far, near)
    places = ((0, 0), (0, 1), (1, 1), (0, 2), (1, 3)), ((2, 2), (2, 3), (3, 3), (2, 1), (3, 0))
    terms = [[[] for _ in range(4)] for _ in stacks]

    def add(third, a, b, block, axis):
        part = stacks[third][:, a * size : (a + 1) * size]
        terms[third][b].append(
            lax.dot_general(
                part,
                block,
                (((1,), (axis,)), ((), ())),
                preferred_element_type=jnp.float32,
            )
        )

    for half_pairs, which in zip(halves, places):
        for third, array in enumerate(thirds(half_pairs)):
            for k, (a, b) in enumerate(which):
                block = array[:, k * size : (k + 1) * size]
                add(third, a, b, block, 0)
                if a != b:
                    add(third, b, a, block, 1)
    p, q, r = (
        jnp.concatenate([tree_sum(t) for t in third], axis=1) for third in terms
    )
    small = p[2 * rows :] + q[rows:] + r
    return (small + (p[rows : 2 * rows] + q[:rows])) + p[:rows]


def to_halves(rows):
    size = rows.shape[-2] // 2
    return jnp.concatenate([rows[..., :size, :], rows[..., size:, :]], axis=-1)


def from_halves(rows, total):
    return jnp.concatenate([rows[..., :total], rows[..., total : 2 * total]], axis=-2)


def my_members(core, members):
    count = members.shape[0] // 2
    return members[pl.ds(pl.multiple_of(core[0] * count, count), count), :]


def own_kernel(core, own, z, out):
    stack = jnp.concatenate([z[:, : own.shape[1]], my_members(core, own)])
    out[...] = product(stack, own[...], 1)


def first_kernel(core, own, far, z, lengths, gram_own, members, out):
    width = own.shape[1]
    total = own.shape[0]
    peers, rows = out.shape[0], 2 * out.shape[1]
    count = peers * rows
    members[:, :width] = own[...]
    members[:, width:] = far[...]
    stack = jnp.concatenate([z[:, width:], my_members(core, far)])
    gram = gram_own[...] + product(stack, far[...], 1)
    raw = 2.0 * A0 * gram[:count] - A0 * A0 * lengths[...]
    out[:, :, : 2 * total] = to_halves(raw.reshape(peers, rows, -1))
    pairs = pack_pairs(core[0] == 0, gram[count:])
    out[:, :, 2 * total :] = pairs.reshape(peers, rows // 2, -1)


def spread_kernel(got, out):
    total = tree_sum([got[i] for i in range(got.shape[0])])
    for i in range(out.shape[0]):
        out[i] = total


def weigh_kernel(scale, members, got, out):
    total = tree_sum([got[i] for i in range(got.shape[0])])
    weights = to_halves(softmax(from_halves(total, members), scale))
    for i in range(out.shape[0]):
        out[i, :, : 2 * members] = weights
        out[i, :, 2 * members :] = total[:, 2 * members :]


def step_kernel(
    got, members, u, noise, angles, lengths, out, y_out, pairs, y_ref, y_sem, pairs_sem
):
    peers, rows = out.shape[0], out.shape[1] // 2
    count = peers * rows
    total, packed = members.shape[0], pairs.shape[2]
    pairs_copy = pltpu.make_async_copy(
        got.at[:, :, pl.ds(2 * total, packed)], pairs, pairs_sem
    )
    pairs_copy.start()
    weights = from_halves(got[...], total).reshape(count, -1)
    blend = product(weights, members[...], 0)
    z = u[...] + GAIN0 * blend
    y = KEEP1 * z + PULL1 * misfit(z, angles[...]) + NOISE1 * noise[...]
    y_ref[...] = y
    y_copy = pltpu.make_async_copy(y_ref, y_out, y_sem)
    y_copy.start()
    gram = product(jnp.concatenate([z, y]), members[...], 1)
    raw1 = 2.0 * A1 * gram[:count] - A1 * A1 * lengths[...]
    raw2 = 2.0 * A2 * gram[count:] - A2 * A2 * lengths[...]
    out[:, :rows, :] = raw1.reshape(peers, rows, -1)
    out[:, rows:, :] = raw2.reshape(peers, rows, -1)
    pairs_copy.wait()
    y_copy.wait()


def weigh_twice_kernel(
    scale1, scale2, core, got, near_in, far_in, out, near, far, near_sem, far_sem
):
    near_copy = pltpu.make_async_copy(near_in, near, near_sem)
    far_copy = pltpu.make_async_copy(far_in, far, far_sem)
    near_copy.start()
    far_copy.start()
    total = tree_sum([got[i] for i in range(got.shape[0])])
    rows = out.shape[1] // 2
    w1 = softmax(total[:rows], scale1)
    for i in range(out.shape[0]):
        out[i, :rows, :] = w1
    near_copy.wait()
    far_copy.wait()
    w1_pairs = times_pairs(core[0] == 0, w1, near[...], far[...])
    w2 = softmax(total[rows:] + (2.0 * A2 * GAIN1) * w1_pairs, scale2)
    for i in range(out.shape[0]):
        out[i, rows:, :] = w2


def last_kernel(first_lane, got, members, y, noise, angles, out):
    peers, rows = got.shape[0], got.shape[1] // 2
    count = peers * rows
    lanes = pl.ds(first_lane, out.shape[1])
    weights = jnp.concatenate(
        [
            got[:, :rows, :].reshape(count, -1),
            got[:, rows:, :].reshape(count, -1),
        ]
    )
    blend = product(weights, members[:, lanes], 0)
    z = y[:, lanes] + GAIN1 * blend[:count]
    z = KEEP2 * z + PULL2 * misfit(z, angles[:, lanes]) + GAIN2 * blend[count:]
    out[...] = z + NOISE2 * noise[:, lanes]


def place_kernel(core, kept, back, out):
    count = kept.shape[0]
    out[pl.ds(pl.multiple_of(core[0] * count, count), count), :] = kept[...]
    out[pl.ds(pl.multiple_of((1 - core[0]) * count, count), count), :] = back[...]


def cut_kernel(array, out, sems):
    width = out.shape[2]
    copies = [
        pltpu.make_async_copy(
            array.at[:, pl.ds(i * width, width)], out.at[i], sems.at[i]
        )
        for i in range(out.shape[0])
    ]
    for copy in copies:
        copy.start()
    for copy in copies:
        copy.wait()


def call(kernel, name, outs, *args, products=1, anywhere=(), scratch=()):
    shapes = tuple(jax.ShapeDtypeStruct(s, jnp.float32) for s in outs)
    result = pl.pallas_call(
        kernel,
        out_shape=shapes,
        in_specs=[
            SMEM if a.dtype == jnp.int32 else ANY if i in anywhere else VMEM
            for i, a in enumerate(args)
        ],
        out_specs=tuple(
            ANY if len(args) + i in anywhere else VMEM for i in range(len(outs))
        ),
        scratch_shapes=list(scratch),
        compiler_params=pltpu.CompilerParams(vmem_limit_bytes=24 << 20),
        cost_estimate=pl.CostEstimate(
            flops=12 * 256 * 512 * 512 * products,
            bytes_accessed=sum(4 * math.prod(s) for s in outs),
            transcendentals=0,
        ),
        name=name,
    )(*args)
    return result if len(outs) > 1 else result[0]


def half(array, which, axis):
    size = array.shape[axis] // 2
    return lax.dynamic_slice_in_dim(array, which * size, size, axis)


def per_device(prior_ensemble, terminal_particles, reverse_perturbation, measured_angles):
    space, mem = lax.axis_size("space"), lax.axis_size("mem")
    core = lax.rem(lax.axis_index("space"), 2)
    core_ref = core.astype(jnp.int32).reshape(1)
    swap = [(i, i ^ 1) for i in range(space)]
    span = mem // DEPTH
    planes = [
        [s * mem + z * span + y for s in range(c, space, 2) for y in range(span)]
        for c in range(2)
        for z in range(DEPTH)
    ]
    columns = [[z * span + y for z in range(DEPTH)] for y in range(span)]
    peers = len(planes[0])

    def other_core(array):
        return lax.ppermute(array, "space", swap)

    def in_plane(blocks):
        return lax.all_to_all(
            blocks, AXES, split_axis=0, concat_axis=0, axis_index_groups=planes
        )

    def in_column(blocks):
        return lax.all_to_all(
            blocks, "mem", split_axis=0, concat_axis=0, axis_index_groups=columns
        )

    temper = math.sqrt(measured_angles.shape[0] * space * mem)
    width = measured_angles.shape[0]
    cut = call(
        cut_kernel,
        "cut",
        [(mem, prior_ensemble.shape[0], width)],
        prior_ensemble,
        anywhere=(0, 1),
        scratch=[DMA((mem,))],
    )
    own = lax.all_to_all(cut, "mem", split_axis=0, concat_axis=0)
    own = own.reshape(mem * prior_ensemble.shape[0], width)
    def pair_up(arrays):
        other = other_core(half(arrays, 1 - core, 1))
        return jnp.concatenate([half(arrays, core, 1), other], axis=-1)

    e1, e2 = pair_up(reverse_perturbation[1:])
    z0, e0 = pair_up(
        jnp.concatenate([terminal_particles[None], reverse_perturbation[:1]])
    )
    angles = jnp.concatenate([measured_angles, other_core(measured_angles)])[None, :]
    u0 = KEEP0 * z0 + PULL0 * misfit(z0, angles) + NOISE0 * e0
    own, z0, u0, e1, e2, angles = lax.optimization_barrier(
        (own, z0, u0, e1, e2, angles)
    )
    far = other_core(own)
    lengths = (jnp.sum(own * own, axis=1) + jnp.sum(far * far, axis=1))[None, :]
    total, width = own.shape
    count = z0.shape[0]
    rows = count // peers
    packed = 5 * total // 4
    mixed = 2 * total + packed
    wide = (peers, 2 * rows, total)
    deep = (DEPTH, 2 * rows, total)

    gram_own = call(own_kernel, "own", [(2 * count, total)], core_ref, own, z0)
    members, blocks = call(
        first_kernel,
        "first",
        [(total, 2 * width), (peers, rows // 2, mixed)],
        core_ref,
        own,
        far,
        z0,
        lengths,
        gram_own,
    )
    blocks = call(
        spread_kernel, "spread", [(DEPTH, rows // 2, mixed)], in_plane(blocks)
    )
    weigh = functools.partial(weigh_kernel, 2.0 * T0 * temper, total)
    blocks = call(weigh, "weigh", [(peers, rows // 2, mixed)], in_column(blocks))
    blocks, y, near = call(
        step_kernel,
        "step",
        [wide, z0.shape, (peers, rows // 2, packed)],
        in_plane(blocks),
        members,
        u0,
        e1,
        angles,
        lengths,
        products=3,
        anywhere=(7, 8),
        scratch=[pltpu.VMEM(z0.shape, jnp.float32), DMA, DMA],
    )
    near = near.reshape(count // 2, packed)
    pairs_far = other_core(near)
    blocks = call(spread_kernel, "spread", [deep], in_plane(blocks))
    weigh = functools.partial(weigh_twice_kernel, 2.0 * T1 * temper, 2.0 * T2 * temper)
    half_pairs = pltpu.VMEM((count // 2, packed), jnp.float32)
    blocks = call(
        weigh,
        "weigh_twice",
        [wide],
        core_ref,
        in_column(blocks),
        near,
        pairs_far,
        anywhere=(2, 3),
        scratch=[half_pairs, half_pairs, DMA, DMA],
    )
    blocks = in_plane(blocks)
    last = functools.partial(last_kernel, width)
    sent = call(last, "last_far", [(count, width)], blocks, members, y, e2, angles)
    back = other_core(sent)
    last = functools.partial(last_kernel, 0)
    kept = call(last, "last_near", [(count, width)], blocks, members, y, e2, angles)
    return call(place_kernel, "place", [(2 * count, width)], core_ref, kept, back)


def solution(mesh):
    in_specs = (
        P("mem", "space"),
        P(None, ("space", "mem")),
        P(None, None, ("space", "mem")),
        P(("space", "mem")),
    )
    out_specs = P(None, ("space", "mem"))
    return jax.shard_map(
        per_device, mesh=mesh, in_specs=in_specs, out_specs=out_specs, check_vma=False
    )
```

```python
import functools
import math

import jax
import jax.numpy as jnp
from jax import lax
from jax.experimental import pallas as pl
from jax.experimental.pallas import tpu as pltpu
from jax.sharding import PartitionSpec as P

ITERS = 3
DEPTH = 4
AXES = ("space", "mem")
VMEM = pl.BlockSpec(memory_space=pltpu.VMEM)
SMEM = pl.BlockSpec(memory_space=pltpu.SMEM)
ANY = pl.BlockSpec(memory_space=pl.ANY)
DMA = pltpu.SemaphoreType.DMA


def constants(step):
    t = 1.0 - step / ITERS
    dt = 1.0 / ITERS
    alpha = 1.0 - 0.5 * t
    drift = -0.5 / alpha
    g2 = 1.0 + t / alpha
    damp = 1.0 - t
    keep = 1.0 - dt * drift - dt * g2 / t
    gain = dt * g2 * alpha / t
    pull = dt * g2 * damp * 4.0
    noise = math.sqrt(dt * g2)
    return alpha, t, keep, gain, pull, noise


A0, T0, KEEP0, GAIN0, PULL0, NOISE0 = constants(0)
A1, T1, KEEP1, GAIN1, PULL1, NOISE1 = constants(1)
A2, T2, KEEP2, GAIN2, PULL2, NOISE2 = constants(2)


def product(a, b, axis):
    return lax.dot_general(
        a,
        b,
        (((1,), (axis,)), ((), ())),
        precision=lax.Precision.HIGHEST,
        preferred_element_type=jnp.float32,
    )


def misfit(z, angles):
    x = jnp.abs(z)
    square = 1.0 + z * z
    far = x > 2.414213562373095
    mid = x > 0.4142135623730951
    num = jnp.where(far, -1.0, jnp.where(mid, x - 1.0, x))
    den = jnp.where(far, x, jnp.where(mid, x + 1.0, 1.0))
    base = jnp.where(far, math.pi / 2, jnp.where(mid, math.pi / 4, 0.0))
    r = 1.0 / (den * square)
    q = num * square * r
    s = q * q
    p = 8.05374449538e-2 * s - 1.38776856032e-1
    p = (p * s + 1.99777106478e-1) * s - 3.33329491539e-1
    y = base + (p * s * q + q)
    return (angles - jnp.where(z < 0.0, -y, y)) * (den * r)


def softmax(raw, scale):
    logits = raw * (1.0 / scale)
    e = jnp.exp(logits - jnp.max(logits, axis=1, keepdims=True))
    return e / jnp.sum(e, axis=1, keepdims=True)


def tree_sum(terms):
    while len(terms) > 1:
        terms = [a + b for a, b in zip(terms[::2], terms[1::2])]
    return terms[0]


def pack_pairs(first, gram):
    rows = gram.shape[0] // 2
    low, high = gram[:rows], gram[rows:]

    def blocks(array, start):
        wrapped = jnp.concatenate([array, array], axis=1)
        return wrapped[:, start * rows : (start + 3) * rows]

    low = jnp.where(first, blocks(low, 0), blocks(low, 2))
    high = jnp.where(first, blocks(high, 1), blocks(high, 3))
    return jnp.concatenate([low, high])


def thirds(array):
    high = array.astype(jnp.bfloat16)
    rest = array - high.astype(jnp.float32)
    mid = rest.astype(jnp.bfloat16)
    return high, mid, (rest - mid.astype(jnp.float32)).astype(jnp.bfloat16)


def times_pairs(first, w, near, far):
    size, rows = near.shape[0] // 2, w.shape[0]
    low, high = w[:, : 2 * size], w[:, 2 * size :]
    w = jnp.where(first, w, jnp.concatenate([high, low], axis=1))
    w_high, w_mid, w_low = thirds(w)
    stacks = (
        jnp.concatenate([w_high, w_mid, w_low]),
        jnp.concatenate([w_high, w_mid]),
        w_high,
    )
    results = []
    packed = [thirds(half_pairs) for half_pairs in (near, far)]
    for third, stack in enumerate(stacks):
        parts = [stack[:, i * size : (i + 1) * size] for i in range(4)]
        sums = [[] for _ in range(4)]
        for i in range(4):
            block = packed[i // 2][third][(i % 2) * size : (i % 2 + 1) * size]
            ahead = lax.dot_general(
                parts[i],
                block,
                (((1,), (0,)), ((), ())),
                preferred_element_type=jnp.float32,
            )
            for k in range(3):
                sums[(i + k) % 4].append(ahead[:, k * size : (k + 1) * size])
            sums[i].append(
                lax.dot_general(
                    parts[(i + 1) % 4],
                    block[:, size : 2 * size],
                    (((1,), (1,)), ((), ())),
                    preferred_element_type=jnp.float32,
                )
            )
        results.append(jnp.concatenate([tree_sum(t) for t in sums], axis=1))
    p, q, r = results
    small = p[2 * rows :] + q[rows:] + r
    total = (small + (p[rows : 2 * rows] + q[:rows])) + p[:rows]
    low, high = total[:, : 2 * size], total[:, 2 * size :]
    return jnp.where(first, total, jnp.concatenate([high, low], axis=1))


def my_members(core, members):
    count = members.shape[0] // 2
    return members[pl.ds(pl.multiple_of(core[0] * count, count), count), :]


def own_kernel(core, own, z, out):
    stack = jnp.concatenate([z[:, : own.shape[1]], my_members(core, own)])
    out[...] = product(stack, own[...], 1)


def first_kernel(core, own, far, z, lengths, gram_own, members, out):
    width = own.shape[1]
    total = own.shape[0]
    peers, rows = out.shape[0], out.shape[1]
    count = peers * rows
    members[:, :width] = own[...]
    members[:, width:] = far[...]
    stack = jnp.concatenate([z[:, width:], my_members(core, far)])
    gram = gram_own[...] + product(stack, far[...], 1)
    raw = 2.0 * A0 * gram[:count] - A0 * A0 * lengths[...]
    out[:, :, :total] = raw.reshape(peers, rows, -1)
    pairs = pack_pairs(core[0] == 0, gram[count:])
    out[:, :, total:] = pairs.reshape(peers, rows, -1)


def spread_kernel(got, out):
    total = tree_sum([got[i] for i in range(got.shape[0])])
    for i in range(out.shape[0]):
        out[i] = total


def weigh_kernel(scale, members, got, out):
    total = tree_sum([got[i] for i in range(got.shape[0])])
    weights = softmax(total[:, :members], scale)
    for i in range(out.shape[0]):
        out[i, :, :members] = weights
        out[i, :, members:] = total[:, members:]


def step_kernel(
    got, members, u, noise, angles, lengths, out, y_out, pairs, y_ref, y_sem, pairs_sem
):
    peers, rows = out.shape[0], out.shape[1] // 2
    count = peers * rows
    total, packed = members.shape[0], pairs.shape[2]
    pairs_copy = pltpu.make_async_copy(
        got.at[:, :, pl.ds(total, packed)], pairs, pairs_sem
    )
    pairs_copy.start()
    blend = product(got[:, :, :total].reshape(count, -1), members[...], 0)
    z = u[...] + GAIN0 * blend
    y = KEEP1 * z + PULL1 * misfit(z, angles[...]) + NOISE1 * noise[...]
    y_ref[...] = y
    y_copy = pltpu.make_async_copy(y_ref, y_out, y_sem)
    y_copy.start()
    gram = product(jnp.concatenate([z, y]), members[...], 1)
    raw1 = 2.0 * A1 * gram[:count] - A1 * A1 * lengths[...]
    raw2 = 2.0 * A2 * gram[count:] - A2 * A2 * lengths[...]
    out[:, :rows, :] = raw1.reshape(peers, rows, -1)
    out[:, rows:, :] = raw2.reshape(peers, rows, -1)
    pairs_copy.wait()
    y_copy.wait()


def weigh_twice_kernel(
    scale1, scale2, core, got, near_in, far_in, out, near, far, near_sem, far_sem
):
    near_copy = pltpu.make_async_copy(near_in, near, near_sem)
    far_copy = pltpu.make_async_copy(far_in, far, far_sem)
    near_copy.start()
    far_copy.start()
    total = tree_sum([got[i] for i in range(got.shape[0])])
    rows = out.shape[1] // 2
    w1 = softmax(total[:rows], scale1)
    for i in range(out.shape[0]):
        out[i, :rows, :] = w1
    near_copy.wait()
    far_copy.wait()
    w1_pairs = times_pairs(core[0] == 0, w1, near[...], far[...])
    w2 = softmax(total[rows:] + (2.0 * A2 * GAIN1) * w1_pairs, scale2)
    for i in range(out.shape[0]):
        out[i, rows:, :] = w2


def last_kernel(first_lane, got, members, y, noise, angles, out):
    peers, rows = got.shape[0], got.shape[1] // 2
    count = peers * rows
    lanes = pl.ds(first_lane, out.shape[1])
    weights = jnp.concatenate(
        [
            got[:, :rows, :].reshape(count, -1),
            got[:, rows:, :].reshape(count, -1),
        ]
    )
    blend = product(weights, members[:, lanes], 0)
    z = y[:, lanes] + GAIN1 * blend[:count]
    z = KEEP2 * z + PULL2 * misfit(z, angles[:, lanes]) + GAIN2 * blend[count:]
    out[...] = z + NOISE2 * noise[:, lanes]


def place_kernel(core, kept, back, out):
    count = kept.shape[0]
    out[pl.ds(pl.multiple_of(core[0] * count, count), count), :] = kept[...]
    out[pl.ds(pl.multiple_of((1 - core[0]) * count, count), count), :] = back[...]


def cut_kernel(array, out, sems):
    width = out.shape[2]
    copies = [
        pltpu.make_async_copy(
            array.at[:, pl.ds(i * width, width)], out.at[i], sems.at[i]
        )
        for i in range(out.shape[0])
    ]
    for copy in copies:
        copy.start()
    for copy in copies:
        copy.wait()


def call(kernel, name, outs, *args, products=1, anywhere=(), scratch=()):
    shapes = tuple(jax.ShapeDtypeStruct(s, jnp.float32) for s in outs)
    result = pl.pallas_call(
        kernel,
        out_shape=shapes,
        in_specs=[
            SMEM if a.dtype == jnp.int32 else ANY if i in anywhere else VMEM
            for i, a in enumerate(args)
        ],
        out_specs=tuple(
            ANY if len(args) + i in anywhere else VMEM for i in range(len(outs))
        ),
        scratch_shapes=list(scratch),
        compiler_params=pltpu.CompilerParams(vmem_limit_bytes=24 << 20),
        cost_estimate=pl.CostEstimate(
            flops=12 * 256 * 512 * 512 * products,
            bytes_accessed=sum(4 * math.prod(s) for s in outs),
            transcendentals=0,
        ),
        name=name,
    )(*args)
    return result if len(outs) > 1 else result[0]


def half(array, which, axis):
    size = array.shape[axis] // 2
    return lax.dynamic_slice_in_dim(array, which * size, size, axis)


def per_device(prior_ensemble, terminal_particles, reverse_perturbation, measured_angles):
    space, mem = lax.axis_size("space"), lax.axis_size("mem")
    core = lax.rem(lax.axis_index("space"), 2)
    core_ref = core.astype(jnp.int32).reshape(1)
    swap = [(i, i ^ 1) for i in range(space)]
    span, pair = 4, mem // 4 // DEPTH
    planes = [
        [
            s * mem + (k * pair + z) * span + y
            for s in range(c, space, 2)
            for z in range(pair)
            for y in range(span)
        ]
        for c in range(2)
        for k in range(DEPTH)
    ]
    columns = [
        [(k * pair + z) * span + y for k in range(DEPTH)]
        for z in range(pair)
        for y in range(span)
    ]
    peers = len(planes[0])

    def other_core(array):
        return lax.ppermute(array, "space", swap)

    def in_plane(blocks):
        return lax.all_to_all(
            blocks, AXES, split_axis=0, concat_axis=0, axis_index_groups=planes
        )

    def in_column(blocks):
        return lax.all_to_all(
            blocks, "mem", split_axis=0, concat_axis=0, axis_index_groups=columns
        )

    temper = math.sqrt(measured_angles.shape[0] * space * mem)
    width = measured_angles.shape[0]
    cut = call(
        cut_kernel,
        "cut",
        [(mem, prior_ensemble.shape[0], width)],
        prior_ensemble,
        anywhere=(0, 1),
        scratch=[DMA((mem,))],
    )
    own = lax.all_to_all(cut, "mem", split_axis=0, concat_axis=0)
    own = own.reshape(mem * prior_ensemble.shape[0], width)
    def pair_up(arrays):
        other = other_core(half(arrays, 1 - core, 1))
        return jnp.concatenate([half(arrays, core, 1), other], axis=-1)

    e1, e2 = pair_up(reverse_perturbation[1:])
    z0, e0 = pair_up(
        jnp.concatenate([terminal_particles[None], reverse_perturbation[:1]])
    )
    angles = jnp.concatenate([measured_angles, other_core(measured_angles)])[None, :]
    u0 = KEEP0 * z0 + PULL0 * misfit(z0, angles) + NOISE0 * e0
    own, z0, u0, e1, e2, angles = lax.optimization_barrier(
        (own, z0, u0, e1, e2, angles)
    )
    far = other_core(own)
    lengths = (jnp.sum(own * own, axis=1) + jnp.sum(far * far, axis=1))[None, :]
    total, width = own.shape
    count = z0.shape[0]
    rows = count // peers
    packed = 3 * total // 4
    wide = (peers, 2 * rows, total)
    deep = (DEPTH, 2 * rows, total)

    gram_own = call(own_kernel, "own", [(2 * count, total)], core_ref, own, z0)
    members, blocks = call(
        first_kernel,
        "first",
        [(total, 2 * width), (peers, rows, total + packed)],
        core_ref,
        own,
        far,
        z0,
        lengths,
        gram_own,
    )
    blocks = call(
        spread_kernel, "spread", [(DEPTH, rows, total + packed)], in_plane(blocks)
    )
    weigh = functools.partial(weigh_kernel, 2.0 * T0 * temper, total)
    blocks = call(weigh, "weigh", [(peers, rows, total + packed)], in_column(blocks))
    blocks, y, near = call(
        step_kernel,
        "step",
        [wide, z0.shape, (peers, rows, packed)],
        in_plane(blocks),
        members,
        u0,
        e1,
        angles,
        lengths,
        products=3,
        anywhere=(7, 8),
        scratch=[pltpu.VMEM(z0.shape, jnp.float32), DMA, DMA],
    )
    near = near.reshape(count, packed)
    pairs_far = other_core(near)
    blocks = call(spread_kernel, "spread", [deep], in_plane(blocks))
    weigh = functools.partial(weigh_twice_kernel, 2.0 * T1 * temper, 2.0 * T2 * temper)
    half_pairs = pltpu.VMEM((count, packed), jnp.float32)
    blocks = call(
        weigh,
        "weigh_twice",
        [wide],
        core_ref,
        in_column(blocks),
        near,
        pairs_far,
        anywhere=(2, 3),
        scratch=[half_pairs, half_pairs, DMA, DMA],
    )
    blocks = in_plane(blocks)
    last = functools.partial(last_kernel, width)
    sent = call(last, "last_far", [(count, width)], blocks, members, y, e2, angles)
    back = other_core(sent)
    last = functools.partial(last_kernel, 0)
    kept = call(last, "last_near", [(count, width)], blocks, members, y, e2, angles)
    return call(place_kernel, "place", [(2 * count, width)], core_ref, kept, back)


def solution(mesh):
    in_specs = (
        P("mem", "space"),
        P(None, ("space", "mem")),
        P(None, None, ("space", "mem")),
        P(("space", "mem")),
    )
    out_specs = P(None, ("space", "mem"))
    return jax.shard_map(
        per_device, mesh=mesh, in_specs=in_specs, out_specs=out_specs, check_vma=False
    )
```

```python
import functools
import math

import jax
import jax.numpy as jnp
from jax import lax
from jax.experimental import pallas as pl
from jax.experimental.pallas import tpu as pltpu
from jax.sharding import PartitionSpec as P

ITERS = 3
DEPTH = 4
AXES = ("space", "mem")
VMEM = pl.BlockSpec(memory_space=pltpu.VMEM)
SMEM = pl.BlockSpec(memory_space=pltpu.SMEM)
ANY = pl.BlockSpec(memory_space=pl.ANY)
DMA = pltpu.SemaphoreType.DMA


def constants(step):
    t = 1.0 - step / ITERS
    dt = 1.0 / ITERS
    alpha = 1.0 - 0.5 * t
    drift = -0.5 / alpha
    g2 = 1.0 + t / alpha
    damp = 1.0 - t
    keep = 1.0 - dt * drift - dt * g2 / t
    gain = dt * g2 * alpha / t
    pull = dt * g2 * damp * 4.0
    noise = math.sqrt(dt * g2)
    return alpha, t, keep, gain, pull, noise


A0, T0, KEEP0, GAIN0, PULL0, NOISE0 = constants(0)
A1, T1, KEEP1, GAIN1, PULL1, NOISE1 = constants(1)
A2, T2, KEEP2, GAIN2, PULL2, NOISE2 = constants(2)


def thirds(array):
    high = array.astype(jnp.bfloat16)
    rest = array - high.astype(jnp.float32)
    mid = rest.astype(jnp.bfloat16)
    return high, mid, (rest - mid.astype(jnp.float32)).astype(jnp.bfloat16)


def product(a, b, axis):
    rows = a.shape[0]
    high, mid, low = thirds(a)

    def one(left, right):
        return lax.dot_general(
            left,
            right,
            (((1,), (axis,)), ((), ())),
            preferred_element_type=jnp.float32,
        )

    b_high, b_mid, b_low = thirds(b)
    p = one(jnp.concatenate([high, mid, low]), b_high)
    q = one(jnp.concatenate([high, mid]), b_mid)
    small = p[2 * rows :] + q[rows:] + one(high, b_low)
    return (small + (p[rows : 2 * rows] + q[:rows])) + p[:rows]


def misfit(z, angles):
    x = jnp.abs(z)
    square = 1.0 + z * z
    far = x > 2.414213562373095
    mid = x > 0.4142135623730951
    num = jnp.where(far, -1.0, jnp.where(mid, x - 1.0, x))
    den = jnp.where(far, x, jnp.where(mid, x + 1.0, 1.0))
    base = jnp.where(far, math.pi / 2, jnp.where(mid, math.pi / 4, 0.0))
    r = 1.0 / (den * square)
    q = num * square * r
    s = q * q
    p = 8.05374449538e-2 * s - 1.38776856032e-1
    p = (p * s + 1.99777106478e-1) * s - 3.33329491539e-1
    y = base + (p * s * q + q)
    return (angles - jnp.where(z < 0.0, -y, y)) * (den * r)


def softmax(raw, scale):
    logits = raw * (1.0 / scale)
    e = jnp.exp(logits - jnp.max(logits, axis=1, keepdims=True))
    return e / jnp.sum(e, axis=1, keepdims=True)


def tree_sum(terms):
    while len(terms) > 1:
        terms = [a + b for a, b in zip(terms[::2], terms[1::2])]
    return terms[0]


def pack_pairs(first, gram):
    rows = gram.shape[0] // 2
    low, high = gram[:rows], gram[rows:]

    def blocks(array, start):
        wrapped = jnp.concatenate([array, array], axis=1)
        return wrapped[:, start * rows : (start + 3) * rows]

    low = jnp.where(first, blocks(low, 0), blocks(low, 2))
    high = jnp.where(first, blocks(high, 1), blocks(high, 3))
    return jnp.concatenate([low, high])


def times_pairs(first, w, near, far):
    size, rows = near.shape[0] // 2, w.shape[0]
    low, high = w[:, : 2 * size], w[:, 2 * size :]
    w = jnp.where(first, w, jnp.concatenate([high, low], axis=1))
    w_high, w_mid, w_low = thirds(w)
    stacks = (
        jnp.concatenate([w_high, w_mid, w_low]),
        jnp.concatenate([w_high, w_mid]),
        w_high,
    )
    results = []
    packed = [thirds(half_pairs) for half_pairs in (near, far)]
    for third, stack in enumerate(stacks):
        parts = [stack[:, i * size : (i + 1) * size] for i in range(4)]
        sums = [[] for _ in range(4)]
        for i in range(4):
            block = packed[i // 2][third][(i % 2) * size : (i % 2 + 1) * size]
            ahead = lax.dot_general(
                parts[i],
                block,
                (((1,), (0,)), ((), ())),
                preferred_element_type=jnp.float32,
            )
            for k in range(3):
                sums[(i + k) % 4].append(ahead[:, k * size : (k + 1) * size])
            sums[i].append(
                lax.dot_general(
                    parts[(i + 1) % 4],
                    block[:, size : 2 * size],
                    (((1,), (1,)), ((), ())),
                    preferred_element_type=jnp.float32,
                )
            )
        results.append(jnp.concatenate([tree_sum(t) for t in sums], axis=1))
    p, q, r = results
    small = p[2 * rows :] + q[rows:] + r
    total = (small + (p[rows : 2 * rows] + q[:rows])) + p[:rows]
    low, high = total[:, : 2 * size], total[:, 2 * size :]
    return jnp.where(first, total, jnp.concatenate([high, low], axis=1))


def my_members(core, members):
    count = members.shape[0] // 2
    return members[pl.ds(pl.multiple_of(core[0] * count, count), count), :]


def own_kernel(core, own, z, out):
    stack = jnp.concatenate([z[:, : own.shape[1]], my_members(core, own)])
    out[...] = product(stack, own[...], 1)


def first_kernel(core, own, far, z, lengths, gram_own, members, out):
    width = own.shape[1]
    total = own.shape[0]
    peers, rows = out.shape[0], out.shape[1]
    count = peers * rows
    members[:, :width] = own[...]
    members[:, width:] = far[...]
    stack = jnp.concatenate([z[:, width:], my_members(core, far)])
    gram = gram_own[...] + product(stack, far[...], 1)
    raw = 2.0 * A0 * gram[:count] - A0 * A0 * lengths[...]
    out[:, :, :total] = raw.reshape(peers, rows, -1)
    pairs = pack_pairs(core[0] == 0, gram[count:])
    out[:, :, total:] = pairs.reshape(peers, rows, -1)


def spread_kernel(got, out):
    total = tree_sum([got[i] for i in range(got.shape[0])])
    for i in range(out.shape[0]):
        out[i] = total


def weigh_kernel(scale, members, got, out):
    total = tree_sum([got[i] for i in range(got.shape[0])])
    weights = softmax(total[:, :members], scale)
    for i in range(out.shape[0]):
        out[i, :, :members] = weights
        out[i, :, members:] = total[:, members:]


def step_kernel(
    got, members, u, noise, angles, lengths, out, y_out, pairs, y_ref, y_sem, pairs_sem
):
    peers, rows = out.shape[0], out.shape[1] // 2
    count = peers * rows
    total, packed = members.shape[0], pairs.shape[2]
    pairs_copy = pltpu.make_async_copy(
        got.at[:, :, pl.ds(total, packed)], pairs, pairs_sem
    )
    pairs_copy.start()
    blend = product(got[:, :, :total].reshape(count, -1), members[...], 0)
    z = u[...] + GAIN0 * blend
    y = KEEP1 * z + PULL1 * misfit(z, angles[...]) + NOISE1 * noise[...]
    y_ref[...] = y
    y_copy = pltpu.make_async_copy(y_ref, y_out, y_sem)
    y_copy.start()
    gram = product(jnp.concatenate([z, y]), members[...], 1)
    raw1 = 2.0 * A1 * gram[:count] - A1 * A1 * lengths[...]
    raw2 = 2.0 * A2 * gram[count:] - A2 * A2 * lengths[...]
    out[:, :rows, :] = raw1.reshape(peers, rows, -1)
    out[:, rows:, :] = raw2.reshape(peers, rows, -1)
    pairs_copy.wait()
    y_copy.wait()


def weigh_twice_kernel(
    scale1, scale2, core, got, near_in, far_in, out, near, far, near_sem, far_sem
):
    near_copy = pltpu.make_async_copy(near_in, near, near_sem)
    far_copy = pltpu.make_async_copy(far_in, far, far_sem)
    near_copy.start()
    far_copy.start()
    total = tree_sum([got[i] for i in range(got.shape[0])])
    rows = out.shape[1] // 2
    w1 = softmax(total[:rows], scale1)
    for i in range(out.shape[0]):
        out[i, :rows, :] = w1
    near_copy.wait()
    far_copy.wait()
    w1_pairs = times_pairs(core[0] == 0, w1, near[...], far[...])
    w2 = softmax(total[rows:] + (2.0 * A2 * GAIN1) * w1_pairs, scale2)
    for i in range(out.shape[0]):
        out[i, rows:, :] = w2


def last_kernel(first_lane, got, members, y, noise, angles, out):
    peers, rows = got.shape[0], got.shape[1] // 2
    count = peers * rows
    lanes = pl.ds(first_lane, out.shape[1])
    weights = jnp.concatenate(
        [
            got[:, :rows, :].reshape(count, -1),
            got[:, rows:, :].reshape(count, -1),
        ]
    )
    blend = product(weights, members[:, lanes], 0)
    z = y[:, lanes] + GAIN1 * blend[:count]
    z = KEEP2 * z + PULL2 * misfit(z, angles[:, lanes]) + GAIN2 * blend[count:]
    out[...] = z + NOISE2 * noise[:, lanes]


def place_kernel(core, kept, back, out):
    count = kept.shape[0]
    out[pl.ds(pl.multiple_of(core[0] * count, count), count), :] = kept[...]
    out[pl.ds(pl.multiple_of((1 - core[0]) * count, count), count), :] = back[...]


def cut_kernel(array, out, sems):
    width = out.shape[2]
    copies = [
        pltpu.make_async_copy(
            array.at[:, pl.ds(i * width, width)], out.at[i], sems.at[i]
        )
        for i in range(out.shape[0])
    ]
    for copy in copies:
        copy.start()
    for copy in copies:
        copy.wait()


def call(kernel, name, outs, *args, products=0, anywhere=(), scratch=()):
    shapes = tuple(jax.ShapeDtypeStruct(s, jnp.float32) for s in outs)
    result = pl.pallas_call(
        kernel,
        out_shape=shapes,
        in_specs=[
            SMEM if a.dtype == jnp.int32 else ANY if i in anywhere else VMEM
            for i, a in enumerate(args)
        ],
        out_specs=tuple(
            ANY if len(args) + i in anywhere else VMEM for i in range(len(outs))
        ),
        scratch_shapes=list(scratch),
        compiler_params=pltpu.CompilerParams(vmem_limit_bytes=24 << 20),
        cost_estimate=pl.CostEstimate(
            flops=12 * 256 * 512 * 512 * products,
            bytes_accessed=sum(4 * math.prod(s) for s in outs),
            transcendentals=0,
        ),
        name=name,
    )(*args)
    return result if len(outs) > 1 else result[0]


def half(array, which, axis):
    size = array.shape[axis] // 2
    return lax.dynamic_slice_in_dim(array, which * size, size, axis)


def per_device(prior_ensemble, terminal_particles, reverse_perturbation, measured_angles):
    space, mem = lax.axis_size("space"), lax.axis_size("mem")
    core = lax.rem(lax.axis_index("space"), 2)
    core_ref = core.astype(jnp.int32).reshape(1)
    swap = [(i, i ^ 1) for i in range(space)]
    span, pair = 4, mem // 4 // DEPTH
    planes = [
        [
            s * mem + (k * pair + z) * span + y
            for z in range(pair)
            for s in range(c, space, 2)
            for y in range(span)
        ]
        for c in range(2)
        for k in range(DEPTH)
    ]
    columns = [
        [(k * pair + z) * span + y for k in range(DEPTH)]
        for z in range(pair)
        for y in range(span)
    ]
    peers = len(planes[0])

    def other_core(array):
        return lax.ppermute(array, "space", swap)

    def in_plane(blocks):
        return lax.all_to_all(
            blocks, AXES, split_axis=0, concat_axis=0, axis_index_groups=planes
        )

    def in_column(blocks):
        return lax.all_to_all(
            blocks, "mem", split_axis=0, concat_axis=0, axis_index_groups=columns
        )

    temper = math.sqrt(measured_angles.shape[0] * space * mem)
    width = measured_angles.shape[0]
    cut = call(
        cut_kernel,
        "cut",
        [(mem, prior_ensemble.shape[0], width)],
        prior_ensemble,
        anywhere=(0, 1),
        scratch=[DMA((mem,))],
    )
    own = lax.all_to_all(cut, "mem", split_axis=0, concat_axis=0)
    own = own.reshape(mem * prior_ensemble.shape[0], width)
    def pair_up(arrays):
        other = other_core(half(arrays, 1 - core, 1))
        return jnp.concatenate([half(arrays, core, 1), other], axis=-1)

    e1, e2 = pair_up(reverse_perturbation[1:])
    z0, e0 = pair_up(
        jnp.concatenate([terminal_particles[None], reverse_perturbation[:1]])
    )
    angles = jnp.concatenate([measured_angles, other_core(measured_angles)])[None, :]
    u0 = KEEP0 * z0 + PULL0 * misfit(z0, angles) + NOISE0 * e0
    own, z0, u0, e1, e2, angles = lax.optimization_barrier(
        (own, z0, u0, e1, e2, angles)
    )
    far = other_core(own)
    lengths = (jnp.sum(own * own, axis=1) + jnp.sum(far * far, axis=1))[None, :]
    total, width = own.shape
    count = z0.shape[0]
    rows = count // peers
    packed = 3 * total // 4
    wide = (peers, 2 * rows, total)
    deep = (DEPTH, 2 * rows, total)

    gram_own = call(own_kernel, "own", [(2 * count, total)], core_ref, own, z0, products=1)
    members, blocks = call(
        first_kernel,
        "first",
        [(total, 2 * width), (peers, rows, total + packed)],
        core_ref,
        own,
        far,
        z0,
        lengths,
        gram_own,
        products=1,
    )
    blocks = call(
        spread_kernel, "spread", [(DEPTH, rows, total + packed)], in_plane(blocks)
    )
    weigh = functools.partial(weigh_kernel, 2.0 * T0 * temper, total)
    blocks = call(weigh, "weigh", [(peers, rows, total + packed)], in_column(blocks))
    blocks, y, near = call(
        step_kernel,
        "step",
        [wide, z0.shape, (peers, rows, packed)],
        in_plane(blocks),
        members,
        u0,
        e1,
        angles,
        lengths,
        products=3,
        anywhere=(7, 8),
        scratch=[pltpu.VMEM(z0.shape, jnp.float32), DMA, DMA],
    )
    near = near.reshape(count, packed)
    pairs_far = other_core(near)
    blocks = call(spread_kernel, "spread", [deep], in_plane(blocks))
    weigh = functools.partial(weigh_twice_kernel, 2.0 * T1 * temper, 2.0 * T2 * temper)
    half_pairs = pltpu.VMEM((count, packed), jnp.float32)
    blocks = call(
        weigh,
        "weigh_twice",
        [wide],
        core_ref,
        in_column(blocks),
        near,
        pairs_far,
        anywhere=(2, 3),
        scratch=[half_pairs, half_pairs, DMA, DMA],
    )
    blocks = in_plane(blocks)
    last = functools.partial(last_kernel, width)
    sent = call(last, "last_far", [(count, width)], blocks, members, y, e2, angles, products=1)
    back = other_core(sent)
    last = functools.partial(last_kernel, 0)
    kept = call(last, "last_near", [(count, width)], blocks, members, y, e2, angles, products=1)
    return call(place_kernel, "place", [(2 * count, width)], core_ref, kept, back)


def solution(mesh):
    in_specs = (
        P("mem", "space"),
        P(None, ("space", "mem")),
        P(None, None, ("space", "mem")),
        P(("space", "mem")),
    )
    out_specs = P(None, ("space", "mem"))
    return jax.shard_map(
        per_device, mesh=mesh, in_specs=in_specs, out_specs=out_specs, check_vma=False
    )
```

```python
import functools
import math

import jax
import jax.numpy as jnp
from jax import lax
from jax.experimental import pallas as pl
from jax.experimental.pallas import tpu as pltpu
from jax.sharding import PartitionSpec as P

ITERS = 3
DEPTH = 4
AXES = ("space", "mem")
VMEM = pl.BlockSpec(memory_space=pltpu.VMEM)
SMEM = pl.BlockSpec(memory_space=pltpu.SMEM)
ANY = pl.BlockSpec(memory_space=pl.ANY)
DMA = pltpu.SemaphoreType.DMA


def constants(step):
    t = 1.0 - step / ITERS
    dt = 1.0 / ITERS
    alpha = 1.0 - 0.5 * t
    drift = -0.5 / alpha
    g2 = 1.0 + t / alpha
    damp = 1.0 - t
    keep = 1.0 - dt * drift - dt * g2 / t
    gain = dt * g2 * alpha / t
    pull = dt * g2 * damp * 4.0
    noise = math.sqrt(dt * g2)
    return alpha, t, keep, gain, pull, noise


A0, T0, KEEP0, GAIN0, PULL0, NOISE0 = constants(0)
A1, T1, KEEP1, GAIN1, PULL1, NOISE1 = constants(1)
A2, T2, KEEP2, GAIN2, PULL2, NOISE2 = constants(2)


def thirds(array):
    high = array.astype(jnp.bfloat16)
    rest = array - high.astype(jnp.float32)
    mid = rest.astype(jnp.bfloat16)
    return high, mid, (rest - mid.astype(jnp.float32)).astype(jnp.bfloat16)


def product(a, b, axis):
    rows = a.shape[0]
    high, mid, low = thirds(a)

    def one(left, right):
        return lax.dot_general(
            left,
            right,
            (((1,), (axis,)), ((), ())),
            preferred_element_type=jnp.float32,
        )

    b_high, b_mid, b_low = thirds(b)
    p = one(jnp.concatenate([high, mid, low]), b_high)
    q = one(jnp.concatenate([high, mid]), b_mid)
    small = p[2 * rows :] + q[rows:] + one(high, b_low)
    return (small + (p[rows : 2 * rows] + q[:rows])) + p[:rows]


def misfit(z, angles):
    x = jnp.abs(z)
    square = 1.0 + z * z
    far = x > 2.414213562373095
    mid = x > 0.4142135623730951
    num = jnp.where(far, -1.0, jnp.where(mid, x - 1.0, x))
    den = jnp.where(far, x, jnp.where(mid, x + 1.0, 1.0))
    base = jnp.where(far, math.pi / 2, jnp.where(mid, math.pi / 4, 0.0))
    r = 1.0 / (den * square)
    q = num * square * r
    s = q * q
    p = 8.05374449538e-2 * s - 1.38776856032e-1
    p = (p * s + 1.99777106478e-1) * s - 3.33329491539e-1
    y = base + (p * s * q + q)
    return (angles - jnp.where(z < 0.0, -y, y)) * (den * r)


def softmax(raw, scale):
    logits = raw * (1.0 / scale)
    e = jnp.exp(logits - jnp.max(logits, axis=1, keepdims=True))
    return e / jnp.sum(e, axis=1, keepdims=True)


def tree_sum(terms):
    while len(terms) > 1:
        terms = [a + b for a, b in zip(terms[::2], terms[1::2])]
    return terms[0]


def pack_pairs(first, gram):
    rows = gram.shape[0] // 2
    low, high = gram[:rows], gram[rows:]

    def blocks(array, start):
        wrapped = jnp.concatenate([array, array], axis=1)
        return wrapped[:, start * rows : (start + 3) * rows]

    low = jnp.where(first, blocks(low, 0), blocks(low, 2))
    high = jnp.where(first, blocks(high, 1), blocks(high, 3))
    return jnp.concatenate([low, high])


def times_pairs(first, w, near, far):
    size, rows = near.shape[0] // 2, w.shape[0]
    low, high = w[:, : 2 * size], w[:, 2 * size :]
    w = jnp.where(first, w, jnp.concatenate([high, low], axis=1))
    w_high, w_mid, w_low = thirds(w)
    stacks = (
        jnp.concatenate([w_high, w_mid, w_low]),
        jnp.concatenate([w_high, w_mid]),
        w_high,
    )
    results = []
    packed = [thirds(half_pairs) for half_pairs in (near, far)]
    for third, stack in enumerate(stacks):
        parts = [stack[:, i * size : (i + 1) * size] for i in range(4)]
        sums = [[] for _ in range(4)]
        for i in range(4):
            block = packed[i // 2][third][(i % 2) * size : (i % 2 + 1) * size]
            ahead = lax.dot_general(
                parts[i],
                block,
                (((1,), (0,)), ((), ())),
                preferred_element_type=jnp.float32,
            )
            for k in range(3):
                sums[(i + k) % 4].append(ahead[:, k * size : (k + 1) * size])
            sums[i].append(
                lax.dot_general(
                    parts[(i + 1) % 4],
                    block[:, size : 2 * size],
                    (((1,), (1,)), ((), ())),
                    preferred_element_type=jnp.float32,
                )
            )
        results.append(jnp.concatenate([tree_sum(t) for t in sums], axis=1))
    p, q, r = results
    small = p[2 * rows :] + q[rows:] + r
    total = (small + (p[rows : 2 * rows] + q[:rows])) + p[:rows]
    low, high = total[:, : 2 * size], total[:, 2 * size :]
    return jnp.where(first, total, jnp.concatenate([high, low], axis=1))


def my_members(core, members):
    count = members.shape[0] // 2
    return members[pl.ds(pl.multiple_of(core[0] * count, count), count), :]


def own_kernel(core, own, z, out):
    stack = jnp.concatenate([z[:, : own.shape[1]], my_members(core, own)])
    out[...] = product(stack, own[...], 1)


def first_kernel(core, own, far, z, lengths, gram_own, members, out):
    width = own.shape[1]
    total = own.shape[0]
    peers, rows = out.shape[0], out.shape[1]
    count = peers * rows
    members[:, :width] = own[...]
    members[:, width:] = far[...]
    stack = jnp.concatenate([z[:, width:], my_members(core, far)])
    gram = gram_own[...] + product(stack, far[...], 1)
    raw = 2.0 * A0 * gram[:count] - A0 * A0 * lengths[...]
    out[:, :, :total] = raw.reshape(peers, rows, -1)
    pairs = pack_pairs(core[0] == 0, gram[count:])
    out[:, :, total:] = pairs.reshape(peers, rows, -1)


def spread_kernel(got, out):
    total = tree_sum([got[i] for i in range(got.shape[0])])
    for i in range(out.shape[0]):
        out[i] = total


def weigh_kernel(scale, members, got, out):
    total = tree_sum([got[i] for i in range(got.shape[0])])
    weights = softmax(total[:, :members], scale)
    for i in range(out.shape[0]):
        out[i, :, :members] = weights
        out[i, :, members:] = total[:, members:]


def step_kernel(
    got, members, u, noise, angles, lengths, out, y_out, pairs, y_ref, y_sem, pairs_sem
):
    peers, rows = out.shape[0], out.shape[1] // 2
    count = peers * rows
    total, packed = members.shape[0], pairs.shape[2]
    pairs_copy = pltpu.make_async_copy(
        got.at[:, :, pl.ds(total, packed)], pairs, pairs_sem
    )
    pairs_copy.start()
    blend = product(got[:, :, :total].reshape(count, -1), members[...], 0)
    z = u[...] + GAIN0 * blend
    y = KEEP1 * z + PULL1 * misfit(z, angles[...]) + NOISE1 * noise[...]
    y_ref[...] = y
    y_copy = pltpu.make_async_copy(y_ref, y_out, y_sem)
    y_copy.start()
    gram = product(jnp.concatenate([z, y]), members[...], 1)
    raw1 = 2.0 * A1 * gram[:count] - A1 * A1 * lengths[...]
    raw2 = 2.0 * A2 * gram[count:] - A2 * A2 * lengths[...]
    out[:, :rows, :] = raw1.reshape(peers, rows, -1)
    out[:, rows:, :] = raw2.reshape(peers, rows, -1)
    pairs_copy.wait()
    y_copy.wait()


def weigh_twice_kernel(
    scale1, scale2, core, got, near_in, far_in, out, near, far, near_sem, far_sem
):
    near_copy = pltpu.make_async_copy(near_in, near, near_sem)
    far_copy = pltpu.make_async_copy(far_in, far, far_sem)
    near_copy.start()
    far_copy.start()
    total = tree_sum([got[i] for i in range(got.shape[0])])
    rows = out.shape[1] // 2
    w1 = softmax(total[:rows], scale1)
    for i in range(out.shape[0]):
        out[i, :rows, :] = w1
    near_copy.wait()
    far_copy.wait()
    w1_pairs = times_pairs(core[0] == 0, w1, near[...], far[...])
    w2 = softmax(total[rows:] + (2.0 * A2 * GAIN1) * w1_pairs, scale2)
    for i in range(out.shape[0]):
        out[i, rows:, :] = w2


def last_kernel(first_lane, got, members, y, noise, angles, out):
    peers, rows = got.shape[0], got.shape[1] // 2
    count = peers * rows
    lanes = pl.ds(first_lane, out.shape[1])
    weights = jnp.concatenate(
        [
            got[:, :rows, :].reshape(count, -1),
            got[:, rows:, :].reshape(count, -1),
        ]
    )
    blend = product(weights, members[:, lanes], 0)
    z = y[:, lanes] + GAIN1 * blend[:count]
    z = KEEP2 * z + PULL2 * misfit(z, angles[:, lanes]) + GAIN2 * blend[count:]
    out[...] = z + NOISE2 * noise[:, lanes]


def place_kernel(core, kept, back, out):
    count = kept.shape[0]
    out[pl.ds(pl.multiple_of(core[0] * count, count), count), :] = kept[...]
    out[pl.ds(pl.multiple_of((1 - core[0]) * count, count), count), :] = back[...]


def cut_kernel(array, out, sems):
    width = out.shape[2]
    copies = [
        pltpu.make_async_copy(
            array.at[:, pl.ds(i * width, width)], out.at[i], sems.at[i]
        )
        for i in range(out.shape[0])
    ]
    for copy in copies:
        copy.start()
    for copy in copies:
        copy.wait()


def call(kernel, name, outs, *args, products=0, anywhere=(), scratch=()):
    shapes = tuple(jax.ShapeDtypeStruct(s, jnp.float32) for s in outs)
    result = pl.pallas_call(
        kernel,
        out_shape=shapes,
        in_specs=[
            SMEM if a.dtype == jnp.int32 else ANY if i in anywhere else VMEM
            for i, a in enumerate(args)
        ],
        out_specs=tuple(
            ANY if len(args) + i in anywhere else VMEM for i in range(len(outs))
        ),
        scratch_shapes=list(scratch),
        compiler_params=pltpu.CompilerParams(vmem_limit_bytes=14 << 20),
        cost_estimate=pl.CostEstimate(
            flops=12 * 256 * 512 * 512 * products,
            bytes_accessed=sum(4 * math.prod(s) for s in outs),
            transcendentals=0,
        ),
        name=name,
    )(*args)
    return result if len(outs) > 1 else result[0]


def half(array, which, axis):
    size = array.shape[axis] // 2
    return lax.dynamic_slice_in_dim(array, which * size, size, axis)


def per_device(prior_ensemble, terminal_particles, reverse_perturbation, measured_angles):
    space, mem = lax.axis_size("space"), lax.axis_size("mem")
    core = lax.rem(lax.axis_index("space"), 2)
    core_ref = core.astype(jnp.int32).reshape(1)
    swap = [(i, i ^ 1) for i in range(space)]
    span, pair = 4, mem // 4 // DEPTH
    planes = [
        [
            s * mem + (k * pair + z) * span + y
            for z in range(pair)
            for s in range(c, space, 2)
            for y in range(span)
        ]
        for c in range(2)
        for k in range(DEPTH)
    ]
    columns = [
        [(k * pair + z) * span + y for k in range(DEPTH)]
        for z in range(pair)
        for y in range(span)
    ]
    peers = len(planes[0])

    def other_core(array):
        return lax.ppermute(array, "space", swap)

    def in_plane(blocks):
        return lax.all_to_all(
            blocks, AXES, split_axis=0, concat_axis=0, axis_index_groups=planes
        )

    def in_column(blocks):
        return lax.all_to_all(
            blocks, "mem", split_axis=0, concat_axis=0, axis_index_groups=columns
        )

    temper = math.sqrt(measured_angles.shape[0] * space * mem)
    width = measured_angles.shape[0]
    cut = call(
        cut_kernel,
        "cut",
        [(mem, prior_ensemble.shape[0], width)],
        prior_ensemble,
        anywhere=(0, 1),
        scratch=[DMA((mem,))],
    )
    own = lax.all_to_all(cut, "mem", split_axis=0, concat_axis=0)
    own = own.reshape(mem * prior_ensemble.shape[0], width)
    def pair_up(arrays):
        other = other_core(half(arrays, 1 - core, 1))
        return jnp.concatenate([half(arrays, core, 1), other], axis=-1)

    e1, e2 = pair_up(reverse_perturbation[1:])
    z0, e0 = pair_up(
        jnp.concatenate([terminal_particles[None], reverse_perturbation[:1]])
    )
    angles = jnp.concatenate([measured_angles, other_core(measured_angles)])[None, :]
    u0 = KEEP0 * z0 + PULL0 * misfit(z0, angles) + NOISE0 * e0
    own, z0, u0, e1, e2, angles = lax.optimization_barrier(
        (own, z0, u0, e1, e2, angles)
    )
    far = other_core(own)
    lengths = (jnp.sum(own * own, axis=1) + jnp.sum(far * far, axis=1))[None, :]
    total, width = own.shape
    count = z0.shape[0]
    rows = count // peers
    packed = 3 * total // 4
    wide = (peers, 2 * rows, total)
    deep = (DEPTH, 2 * rows, total)

    gram_own = call(own_kernel, "own", [(2 * count, total)], core_ref, own, z0, products=1)
    members, blocks = call(
        first_kernel,
        "first",
        [(total, 2 * width), (peers, rows, total + packed)],
        core_ref,
        own,
        far,
        z0,
        lengths,
        gram_own,
        products=1,
    )
    blocks = call(
        spread_kernel, "spread", [(DEPTH, rows, total + packed)], in_plane(blocks)
    )
    weigh = functools.partial(weigh_kernel, 2.0 * T0 * temper, total)
    blocks = call(weigh, "weigh", [(peers, rows, total + packed)], in_column(blocks))
    blocks, y, near = call(
        step_kernel,
        "step",
        [wide, z0.shape, (peers, rows, packed)],
        in_plane(blocks),
        members,
        u0,
        e1,
        angles,
        lengths,
        products=3,
        anywhere=(7, 8),
        scratch=[pltpu.VMEM(z0.shape, jnp.float32), DMA, DMA],
    )
    near = near.reshape(count, packed)
    pairs_far = other_core(near)
    blocks = call(spread_kernel, "spread", [deep], in_plane(blocks))
    weigh = functools.partial(weigh_twice_kernel, 2.0 * T1 * temper, 2.0 * T2 * temper)
    half_pairs = pltpu.VMEM((count, packed), jnp.float32)
    blocks = call(
        weigh,
        "weigh_twice",
        [wide],
        core_ref,
        in_column(blocks),
        near,
        pairs_far,
        anywhere=(2, 3),
        scratch=[half_pairs, half_pairs, DMA, DMA],
    )
    blocks = in_plane(blocks)
    last = functools.partial(last_kernel, width)
    sent = call(last, "last_far", [(count, width)], blocks, members, y, e2, angles, products=1)
    back = other_core(sent)
    last = functools.partial(last_kernel, 0)
    kept = call(last, "last_near", [(count, width)], blocks, members, y, e2, angles, products=1)
    return call(place_kernel, "place", [(2 * count, width)], core_ref, kept, back)


def solution(mesh):
    in_specs = (
        P("mem", "space"),
        P(None, ("space", "mem")),
        P(None, None, ("space", "mem")),
        P(("space", "mem")),
    )
    out_specs = P(None, ("space", "mem"))
    return jax.shard_map(
        per_device, mesh=mesh, in_specs=in_specs, out_specs=out_specs, check_vma=False
    )
```
